32 devices in a mesh: gz: 2 (over core), row: 4 (over y, x), col: 4 (over z).
Axes of the slice: x: 2, y: 2, z: 4, core: 2. Of those that a mesh axis runs over, the one named last changes fastest.
Arguments:
- l_panel: float32 [2, 8, 4, 8, 128, 256], P('gz', None, 'row', 'col'), may hold values from -6 to 6
- l_rows: int32 [2, 8, 4, 8], P('gz', None, 'row'), may hold values from -1 to 7, as said below
- u_panel: float32 [2, 8, 4, 16, 256, 128], P('gz', None, 'col', 'row'), may hold values from -0.125 to 0.125
- u_cols: int32 [2, 8, 4, 16], P('gz', None, 'col'), may hold values from -1 to 15, as said below
- u11_inv: float32 [2, 8, 256, 256], P('gz'), as said below
- ancestor: float32 [4, 1024, 8192], P('row', 'gz', 'col'), may hold values from -6 to 6
Outputs:
- schur: float32 [4, 1024, 8192], P('row', 'gz', 'col')
The draws below stay inside these ranges and needn't reach their ends.
Inputs may be any that keep to these rules, and one draw needn't show every extreme that they name: `l_rows`: within one layer, supernode and process row the live entries are distinct; at most 8 are live, and in every layer and process row some supernode has all 8 live. `u_cols`: within one layer, supernode and process column the live entries are distinct; at most 16 are live, and in every layer and process column some supernode has all 16 live. `u11_inv`: upper triangular, with diagonal entries between 0.5 and 1.5.
All inputs are finite; a program needn't handle non-finite values.
Results may differ from the reference program's by a relative error of at most 0.000058.
Values sent between devices are 32-bit elements; how exact they have to be, the bound alone decides.
No kernel may reach another device: no remote copies, remote signals or barrier semaphores. Data moves between devices by JAX's collectives and lax.ppermute only.
A program may use at most 128 MiB of HBM per device.

```python
import math
import jax
import jax.numpy as jnp
from jax import lax

W = 256
B = 128
SN = 8
AR = 8
AC = 16
LS = 2
US = 4
N_GZ = 2
N_ROW = 4
N_COL = 4


def slot_targets(key, leading, slots, largest):
    rank_key, value_key, live_key, full_key = jax.random.split(key, 4)
    positions = jnp.arange(slots, dtype=jnp.int32)
    rank_score = jax.random.randint(rank_key, leading + (slots,), 0, 1 << 20) * slots + positions
    ranks = jnp.argsort(jnp.argsort(rank_score, axis=-1), axis=-1).astype(jnp.int32)
    value_score = jax.random.randint(value_key, leading + (largest,), 0, 1 << 20) * largest + jnp.arange(largest, dtype=jnp.int32)
    values_perm = jnp.argsort(value_score, axis=-1).astype(jnp.int32)
    picked = jnp.take_along_axis(values_perm, jnp.minimum(ranks, largest - 1), axis=-1)
    live_count = jax.random.randint(live_key, leading, (largest + 1) // 2, largest + 1)
    full_pick = jax.random.randint(full_key, (leading[0], 1, leading[2]), 0, leading[1])
    supernodes = jnp.arange(leading[1], dtype=jnp.int32)[None, :, None]
    live_count = jnp.where(supernodes == full_pick, largest, live_count)
    return jnp.where(ranks < live_count[..., None], picked, -1).astype(jnp.int32)


def draw_l_rows(key, part):
    return slot_targets(jax.random.fold_in(key, 11), (N_GZ, SN, N_ROW), N_COL * LS, AR)


def draw_u_cols(key, part):
    return slot_targets(jax.random.fold_in(key, 23), (N_GZ, SN, N_COL), N_ROW * US, AC)


def draw_u11_inv(key, part):
    off_key, diag_key = jax.random.split(jax.random.fold_in(key, 37))
    shape = (N_GZ, SN, W, W)
    row_index = jnp.arange(W)[:, None]
    col_index = jnp.arange(W)[None, :]
    upper = (col_index > row_index).astype(jnp.float32)
    diagonal = (col_index == row_index).astype(jnp.float32)
    off_part = jax.random.normal(off_key, shape, jnp.float32) * (0.6 / math.sqrt(W))
    diag_part = jax.random.uniform(diag_key, shape, jnp.float32, 0.5, 1.5)
    return (off_part * upper + diag_part * diagonal).astype(jnp.float32)


def block_scale(key, shape, pieces, least, top_value):
    loudness, own = 1.0, jax.random.fold_in(key, 6)
    for dim, shards_of in pieces:
        steps = jnp.exp(jax.random.uniform(jax.random.fold_in(own, dim), (shards_of,), jnp.float32, least / len(pieces), top_value / len(pieces)))
        loudness = loudness * jnp.repeat(steps, shape[dim] // shards_of).reshape([-1 if axis == dim else 1 for axis in range(len(shape))])
    return loudness


def centred(stream_key, extent, deviation, most, cuts=(), kind=jnp.bfloat16):
    values = deviation * jax.random.normal(stream_key, extent, jnp.float32)
    if cuts:
        values = values * block_scale(stream_key, extent, cuts, -0.22, 0.18)
    return jnp.clip(values, -most, most).astype(kind)


def setup_inputs(seed: int = 0) -> dict:
    keys = jax.random.split(jax.random.key(seed), 7)
    l_panel = centred(keys[0], (N_GZ, SN, N_ROW, N_COL * LS, B, W), 1.0, 6.0, ((0, 2), (2, 4), (3, 4)), jnp.float32)
    l_rows = draw_l_rows(jax.random.fold_in(keys[6], 71), 0)
    u_panel = centred(keys[2], (N_GZ, SN, N_COL, N_ROW * US, W, B), (SN * W) ** -0.5, 0.125, ((0, 2), (2, 4), (3, 4)), jnp.float32)
    u_cols = draw_u_cols(jax.random.fold_in(keys[6], 71), 0)
    u11_inv = draw_u11_inv(jax.random.fold_in(keys[6], 71), 0)
    ancestor = centred(keys[5], (N_ROW, AR * B, N_COL * AC * B), 1.0, 6.0, ((0, 4), (1, 2), (2, 4)), jnp.float32)
    return dict(l_panel=l_panel, l_rows=l_rows, u_panel=u_panel, u_cols=u_cols, u11_inv=u11_inv, ancestor=ancestor)


highest = lax.Precision.HIGHEST


def reference(l_panel, l_rows, u_panel, u_cols, u11_inv, ancestor):
    l_scaled = jnp.einsum("gsrkbw,gswv->gsrkbv", l_panel, u11_inv, precision=highest)
    l_onehot = (l_rows[..., None, :] == jnp.arange(AR, dtype=jnp.int32)[:, None]).astype(jnp.float32)
    l_placed = jnp.einsum("gsrak,gsrkbw->grabsw", l_onehot, l_scaled, precision=highest)
    u_onehot = (u_cols[..., None, :] == jnp.arange(AC, dtype=jnp.int32)[:, None]).astype(jnp.float32)
    u_placed = jnp.einsum("gscak,gsckwb->gcswab", u_onehot, u_panel, precision=highest)
    l_matrix = l_placed.reshape(N_GZ, N_ROW, AR * B, SN * W)
    u_matrix = u_placed.reshape(N_GZ, N_COL, SN * W, AC * B)

    def row_update(row_panel):
        product = jnp.einsum("gxk,gcky->xcy", row_panel, u_matrix, precision=highest)
        return product.reshape(AR * B, N_COL * AC * B)

    update = lax.map(row_update, jnp.moveaxis(l_matrix, 1, 0))
    return ancestor - update
```

```python
import functools

import jax
import jax.numpy as jnp
from jax import lax
from jax.experimental import pallas as pl
from jax.experimental.pallas import tpu as pltpu
from jax.sharding import PartitionSpec as P

W = 256
B = 128
AR = 8
AC = 16
HALF = AR * B // 2
F32 = jnp.float32
BF16 = jnp.bfloat16


def split(x):
    hi = x.astype(BF16)
    return hi, (x - hi.astype(F32)).astype(BF16)


def dot(a, b):
    return jnp.dot(a, b, preferred_element_type=F32)


def update_kernel(n_l, n_u, start, has_send, l_tgt, u_tgt, l_base, u_base, *refs):
    l_refs, refs = refs[:n_l], refs[n_l:]
    u_refs, refs = refs[:n_u], refs[n_u:]
    inv_ref, keep_in, refs = refs[0], refs[1], refs[2:]
    if has_send:
        send_in, refs = refs[0], refs[1:]
    send, keep, raw_h, raw_l, l_cat, u_cat = refs
    step = pl.program_id(0)
    node = start + step

    @pl.when(step == 0)
    def _():
        keep[...] = keep_in[...]
        send[...] = send_in[...] if has_send else jnp.zeros_like(send)

    raw_h[...] = jnp.zeros_like(raw_h)
    raw_l[...] = jnp.zeros_like(raw_l)
    for b, ref in enumerate(l_refs):
        base = l_base[b]
        for j in range(ref.shape[1]):
            tgt = jnp.where(base >= 0, l_tgt[node, jnp.maximum(base, 0) + j], -1)

            @pl.when(tgt >= 0)
            def _(ref=ref, j=j, tgt=tgt):
                rows = pl.ds(pl.multiple_of(tgt * B, B), B)
                hi, lo = split(ref[0, j])
                raw_h[rows, :] = hi
                raw_l[rows, :] = lo

    inv_h, inv_l = split(inv_ref[0])
    for m in range(0, AR * B, 256):
        rh, rl = raw_h[m : m + 256, :], raw_l[m : m + 256, :]
        hi, lo = split(dot(rh, inv_h) + dot(rh, inv_l) + dot(rl, inv_h))
        l_cat[m : m + 256, 0:W] = hi
        l_cat[m : m + 256, W : 2 * W] = lo
        l_cat[m : m + 256, 2 * W : 3 * W] = hi

    for b, ref in enumerate(u_refs):
        base = u_base[b]
        for j in range(0, ref.shape[1], 2):
            tgts = [u_tgt[node, base + j], u_tgt[node, base + j + 1]]

            @pl.when(jnp.maximum(tgts[0], tgts[1]) >= 0)
            def _(ref=ref, j=j, tgts=tgts):
                cols = []
                for i, tgt in enumerate(tgts):
                    hi, lo = split(jnp.where(tgt >= 0, ref[0, j + i], 0.0))
                    here = slice(i * B, (i + 1) * B)
                    u_cat[0:W, here] = hi
                    u_cat[W : 2 * W, here] = hi
                    u_cat[2 * W : 3 * W, here] = lo
                    cols.append(pl.ds(pl.multiple_of(jnp.maximum(tgt, 0) * B, B), B))
                part = dot(l_cat[0:HALF, :], u_cat[...])
                send[:, cols[0]] += part[:, :B]
                send[:, cols[1]] += part[:, B:]
                part = dot(l_cat[HALF : 2 * HALF, :], u_cat[...])
                keep[:, cols[0]] -= part[:, :B]
                keep[:, cols[1]] -= part[:, B:]


def apply_update(start, tables, l_bufs, u_bufs, u11_inv, send, keep):
    nodes = l_bufs[0].shape[0]
    width = keep.shape[1]

    def per_node(buf):
        return pl.BlockSpec((1,) + buf.shape[1:], lambda s, *_: (s, 0, 0, 0))

    whole = pl.BlockSpec((HALF, width), lambda s, *_: (0, 0), pipeline_mode=pl.Buffered(1))
    acc = jax.ShapeDtypeStruct((HALF, width), F32)
    sends = [] if send is None else [send]
    n_in = 4 + len(l_bufs) + len(u_bufs)
    return pl.pallas_call(
        functools.partial(update_kernel, len(l_bufs), len(u_bufs), start, bool(sends)),
        out_shape=(acc, acc),
        grid_spec=pltpu.PrefetchScalarGridSpec(
            num_scalar_prefetch=4,
            grid=(nodes,),
            in_specs=[per_node(b) for b in l_bufs]
            + [per_node(b) for b in u_bufs]
            + [pl.BlockSpec((1, W, W), lambda s, *_: (start + s, 0, 0))]
            + [whole] * (1 + len(sends)),
            out_specs=(whole, whole),
            scratch_shapes=[
                pltpu.VMEM((AR * B, W), BF16),
                pltpu.VMEM((AR * B, W), BF16),
                pltpu.VMEM((AR * B, 3 * W), BF16),
                pltpu.VMEM((3 * W, 2 * B), BF16),
            ],
        ),
        input_output_aliases={n_in + 1: 1, n_in + 2: 0} if sends else {},
        compiler_params=pltpu.CompilerParams(
            dimension_semantics=("arbitrary",), vmem_limit_bytes=48 << 20
        ),
    )(*tables, *l_bufs, *u_bufs, u11_inv, keep, *sends)


class Link:
    def __init__(self, axis):
        self.axis, self.last = axis, None

    def send(self, x, pairs):
        if self.last is not None:
            x, _ = lax.optimization_barrier((x, self.last))
        self.last = lax.ppermute(x, self.axis, pairs)
        return self.last


def up(hop):
    return [(z, z + 1) for z in range(hop - 1, 3)]


def down(hop):
    return [(z, z - 1) for z in range(1, 5 - hop)]


def side(mask):
    return [(r, r ^ mask) for r in range(4)]


def exchange(l_chunk, u_h0, u_h1, links):
    lx, ly, lu, ld = links
    x0, y1 = lx.send(u_h0, side(1)), ly.send(u_h1, side(2))
    up1, down1 = lu.send(l_chunk, up(1)), ld.send(l_chunk, down(1))
    x1, y0 = lx.send(u_h1, side(1)), ly.send(u_h0, side(2))
    up2, down2 = lu.send(up1, up(2)), ld.send(down1, down(2))
    d1, d0 = lx.send(y1, side(1)), ly.send(x0, side(2))
    up3, down3 = lu.send(up2, up(3)), ld.send(down2, down(3))
    l_bufs = [l_chunk, up1, down1, up2, down2, up3, down3]
    u_bufs = [u_h0, u_h1, x0, x1, y0, y1, d0, d1]
    return l_bufs, u_bufs


def body(rows, cols, l_panel, l_rows, u_panel, u_cols, u11_inv, ancestor):
    gz, row, col = (lax.axis_index(a) for a in ("gz", "row", "col"))
    l_own, u_own, inv = l_panel[0, :, 0], u_panel[0, :, 0], u11_inv[0]
    nodes, l_slots = l_own.shape[:2]
    u_slots = u_own.shape[1]
    l_tgt = l_rows[0, :, 0]
    l_tgt = jnp.where(l_tgt < 0, -1, (l_tgt + (AR // 2) * (1 - gz)) % AR)
    u_tgt = u_cols[0, :, 0]
    keep, send = ancestor[0], None

    if rows == 4 and cols == 4:
        half = u_slots // 2
        sources = jnp.stack([col, col - 1, col + 1, col - 2, col + 2, col - 3, col + 3])
        l_base = jnp.where((sources >= 0) & (sources < cols), sources * l_slots, -1)
        squares = jnp.stack([row, row, row ^ 1, row ^ 1, row ^ 2, row ^ 2, row ^ 3, row ^ 3])
        u_base = squares * u_slots + half * (jnp.arange(8, dtype=jnp.int32) % 2)
        tables = [t.astype(jnp.int32) for t in (l_tgt, u_tgt, l_base, u_base)]
        links = [Link("row"), Link("row"), Link("col"), Link("col")]
        size = nodes // 2
        for start in range(0, nodes, size):
            here = slice(start, start + size)
            l_bufs, u_bufs = exchange(l_own[here], u_own[here, :half], u_own[here, half:], links)
            send, keep = apply_update(start, tables, l_bufs, u_bufs, inv, send, keep)
    else:
        l_all = lax.all_gather(l_own, "col", axis=1, tiled=True)
        u_all = lax.all_gather(u_own, "row", axis=1, tiled=True)
        zero = jnp.zeros((1,), jnp.int32)
        tables = [t.astype(jnp.int32) for t in (l_tgt, u_tgt, zero, zero)]
        send, keep = apply_update(0, tables, [l_all], [u_all], inv, send, keep)

    other = lax.ppermute(send, "gz", [(0, 1), (1, 0)])
    return (keep - other)[None]


def solution(mesh):
    in_specs = (
        P("gz", None, "row", "col", None, None),
        P("gz", None, "row", None),
        P("gz", None, "col", "row", None, None),
        P("gz", None, "col", None),
        P("gz", None, None, None),
        P("row", "gz", "col"),
    )
    return jax.shard_map(
        functools.partial(body, mesh.shape["row"], mesh.shape["col"]),
        mesh=mesh,
        in_specs=in_specs,
        out_specs=P("row", "gz", "col"),
        check_vma=False,
    )
```

```python
import functools

import jax
import jax.numpy as jnp
from jax import lax
from jax.experimental import pallas as pl
from jax.experimental.pallas import tpu as pltpu
from jax.sharding import PartitionSpec as P

W = 256
B = 128
AR = 8
AC = 16
HALF = AR * B // 2
F32 = jnp.float32
BF16 = jnp.bfloat16


def split(x):
    hi = x.astype(BF16)
    return hi, (x - hi.astype(F32)).astype(BF16)


def dot(a, b):
    return jnp.dot(a, b, preferred_element_type=F32)


def update_kernel(n_l, n_u, start, first, l_tgt, u_tgt, l_base, u_base, *refs):
    l_refs, refs = refs[:n_l], refs[n_l:]
    u_refs, refs = refs[:n_u], refs[n_u:]
    inv_ref, keep_in, _, send, keep, token, raw_h, raw_l, l_cat, u_cat = refs
    step = pl.program_id(0)
    node = start + step

    @pl.when(step == 0)
    def _():
        token[...] = jnp.zeros_like(token)
        if first:
            keep[...] = keep_in[...]
            send[...] = jnp.zeros_like(send)

    raw_h[...] = jnp.zeros_like(raw_h)
    raw_l[...] = jnp.zeros_like(raw_l)
    for b, ref in enumerate(l_refs):
        base = l_base[b]
        for j in range(ref.shape[1]):
            tgt = jnp.where(base >= 0, l_tgt[node, jnp.maximum(base, 0) + j], -1)

            @pl.when(tgt >= 0)
            def _(ref=ref, j=j, tgt=tgt):
                rows = pl.ds(pl.multiple_of(tgt * B, B), B)
                hi, lo = split(ref[0, j])
                raw_h[rows, :] = hi
                raw_l[rows, :] = lo

    inv_h, inv_l = split(inv_ref[0])
    for m in range(0, AR * B, 256):
        rh, rl = raw_h[m : m + 256, :], raw_l[m : m + 256, :]
        hi, lo = split(dot(rh, inv_h) + dot(rh, inv_l) + dot(rl, inv_h))
        l_cat[m : m + 256, 0:W] = hi
        l_cat[m : m + 256, W : 2 * W] = lo

    u_cat[...] = jnp.zeros_like(u_cat)
    for b, ref in enumerate(u_refs):
        base = u_base[b]
        for j in range(ref.shape[1]):
            tgt = u_tgt[node, base + j]

            @pl.when(tgt >= 0)
            def _(ref=ref, j=j, tgt=tgt):
                cols = pl.ds(pl.multiple_of(tgt * B, B), B)
                hi, lo = split(ref[0, j])
                u_cat[0:W, cols] = hi
                u_cat[W : 2 * W, cols] = lo

    uh, ul = u_cat[0:W, :], u_cat[W : 2 * W, :]

    def product(rows):
        lh, ll = l_cat[rows, 0:W], l_cat[rows, W : 2 * W]
        return dot(lh, uh) + dot(ll, uh) + dot(lh, ul)

    send[...] += product(slice(0, HALF))
    keep[...] -= product(slice(HALF, 2 * HALF))


def apply_update(nodes, offsets, tables, l_bufs, u_bufs, u11_inv, send, keep):
    start, stop = nodes
    width = keep.shape[1]
    first = send is None

    def per_node(buf, offset):
        return pl.BlockSpec((1,) + buf.shape[1:], lambda s, *_: (offset + s, 0, 0, 0))

    vmem = pl.BlockSpec(memory_space=pltpu.VMEM)
    acc = pltpu.VMEM((HALF, width), F32)
    n_in = 4 + len(l_bufs) + len(u_bufs)
    last = jnp.zeros((8, 128), F32) if first else send
    l_bufs, u_bufs = ([pltpu.with_memory_space_constraint(b, pltpu.HBM) for b in bufs] for bufs in (l_bufs, u_bufs))
    return pl.pallas_call(
        functools.partial(update_kernel, len(l_bufs), len(u_bufs), start, first),
        out_shape=(acc, acc, jax.ShapeDtypeStruct((8, 128), F32)),
        grid_spec=pltpu.PrefetchScalarGridSpec(
            num_scalar_prefetch=4,
            grid=(stop - start,),
            in_specs=[per_node(b, o) for b, o in zip([*l_bufs, *u_bufs], offsets)]
            + [pl.BlockSpec((1, W, W), lambda s, *_: (start + s, 0, 0)), vmem, vmem],
            out_specs=(vmem, vmem, vmem),
            scratch_shapes=[
                pltpu.VMEM((AR * B, W), BF16),
                pltpu.VMEM((AR * B, W), BF16),
                pltpu.VMEM((AR * B, 2 * W), BF16),
                pltpu.VMEM((2 * W, AC * B), BF16),
            ],
        ),
        input_output_aliases={} if first else {n_in + 1: 1, n_in + 2: 0},
        compiler_params=pltpu.CompilerParams(
            dimension_semantics=("arbitrary",), vmem_limit_bytes=32 << 20
        ),
    )(*tables, *l_bufs, *u_bufs, u11_inv, keep, last)


class Link:
    def __init__(self, axis):
        self.axis, self.after = axis, []

    def send(self, x, pairs):
        if self.after:
            x = lax.optimization_barrier((x, *self.after))[0]
        out = lax.ppermute(x, self.axis, pairs)
        self.after = [out]
        return out


def up(hop):
    return [(z, z + 1) for z in range(hop - 1, 3)]


def down(hop):
    return [(z, z - 1) for z in range(1, 5 - hop)]


def side(mask):
    return [(r, r ^ mask) for r in range(4)]


def hold(links, token):
    for link in links:
        link.after.append(token)


class Exchange:
    def __init__(self, links, l_chunk, u_h0, u_h1):
        self.links = links
        self.l, self.h = l_chunk, (u_h0, u_h1)

    def first(self):
        lx, ly, lu, ld = self.links
        self.u1, self.d1 = lu.send(self.l, up(1)), ld.send(self.l, down(1))
        self.x0, self.y1 = lx.send(self.h[0], side(1)), ly.send(self.h[1], side(2))

    def second(self):
        lx, ly, lu, ld = self.links
        self.u2, self.d2 = lu.send(self.u1, up(2)), ld.send(self.d1, down(2))
        self.x1, self.y0 = lx.send(self.h[1], side(1)), ly.send(self.h[0], side(2))

    def third(self, here):
        lx, ly, lu, ld = self.links
        u3, d3 = lu.send(self.u2[here], up(3)), ld.send(self.d2[here], down(3))
        f1, f0 = lx.send(self.y1[here], side(1)), ly.send(self.x0[here], side(2))
        return (u3, d3), (f0, f1)

    def buffers(self, third):
        l_bufs = [self.l, self.u1, self.d1, self.u2, self.d2, *third[0]]
        u_bufs = [*self.h, self.x0, self.x1, self.y0, self.y1, *third[1]]
        return l_bufs, u_bufs


def body(rows, cols, l_panel, l_rows, u_panel, u_cols, u11_inv, ancestor):
    gz, row, col = (lax.axis_index(a) for a in ("gz", "row", "col"))
    l_own, u_own, inv = l_panel[0, :, 0], u_panel[0, :, 0], u11_inv[0]
    nodes, l_slots = l_own.shape[:2]
    u_slots = u_own.shape[1]
    l_tgt = l_rows[0, :, 0]
    l_tgt = jnp.where(l_tgt < 0, -1, (l_tgt + (AR // 2) * (1 - gz)) % AR)
    u_tgt = u_cols[0, :, 0]
    keep, send = ancestor[0], None

    if rows == 4 and cols == 4:
        half = u_slots // 2
        sources = jnp.stack([col, col - 1, col + 1, col - 2, col + 2, col - 3, col + 3])
        l_base = jnp.where((sources >= 0) & (sources < cols), sources * l_slots, -1)
        squares = jnp.stack([row, row, row ^ 1, row ^ 1, row ^ 2, row ^ 2, row ^ 3, row ^ 3])
        u_base = squares * u_slots + half * (jnp.arange(8, dtype=jnp.int32) % 2)
        tables = [t.astype(jnp.int32) for t in (l_tgt, u_tgt, l_base, u_base)]
        links = [Link("row"), Link("row"), Link("col"), Link("col")]
        size, part = nodes // 2, nodes // 4
        chunks = []
        for start in (0, size):
            here = slice(start, start + size)
            chunks.append(Exchange(links, l_own[here], u_own[here, :half], u_own[here, half:]))
        one, two = chunks

        one.first()
        one.second()
        bufs = one.buffers(one.third(slice(0, size)))
        two.first()
        send, keep, token = apply_update((0, part), [0] * 15, tables, *bufs, inv, send, keep)
        hold(links, token)
        two.second()
        send, keep, token = apply_update((part, size), [part] * 15, tables, *bufs, inv, send, keep)
        hold(links, token)
        for k in range(2):
            bufs = two.buffers(two.third(slice(k * part, (k + 1) * part)))
            at = [k * part] * 5 + [0] * 2 + [k * part] * 6 + [0] * 2
            nodes_now = (size + k * part, size + (k + 1) * part)
            send, keep, token = apply_update(nodes_now, at, tables, *bufs, inv, send, keep)
    else:
        l_all = lax.all_gather(l_own, "col", axis=1, tiled=True)
        u_all = lax.all_gather(u_own, "row", axis=1, tiled=True)
        zero = jnp.zeros((1,), jnp.int32)
        tables = [t.astype(jnp.int32) for t in (l_tgt, u_tgt, zero, zero)]
        send, keep, _ = apply_update((0, nodes), [0, 0], tables, [l_all], [u_all], inv, send, keep)

    other = lax.ppermute(send, "gz", [(0, 1), (1, 0)])
    return (keep - other)[None]


def solution(mesh):
    in_specs = (
        P("gz", None, "row", "col", None, None),
        P("gz", None, "row", None),
        P("gz", None, "col", "row", None, None),
        P("gz", None, "col", None),
        P("gz", None, None, None),
        P("row", "gz", "col"),
    )
    return jax.shard_map(
        functools.partial(body, mesh.shape["row"], mesh.shape["col"]),
        mesh=mesh,
        in_specs=in_specs,
        out_specs=P("row", "gz", "col"),
        check_vma=False,
    )
```

```python
import functools

import jax
import jax.numpy as jnp
from jax import lax
from jax.experimental import pallas as pl
from jax.experimental.pallas import tpu as pltpu
from jax.sharding import PartitionSpec as P

W = 256
B = 128
AR = 8
AC = 16
HALF = AR * B // 2
F32 = jnp.float32
BF16 = jnp.bfloat16


def split(x):
    hi = x.astype(BF16)
    return hi, (x - hi.astype(F32)).astype(BF16)


def dot(a, b):
    return jnp.dot(a, b, preferred_element_type=F32)


def slot_rows(l_tgt, l_base, node, b, j):
    base = l_base[b]
    return jnp.where(base >= 0, l_tgt[node, jnp.maximum(base, 0) + j], -1)


def block(tgt):
    return pl.ds(pl.multiple_of(tgt * B, B), B)


def scale(hi, lo, inv):
    return split(dot(hi, inv[0]) + dot(hi, inv[1]) + dot(lo, inv[0]))


def place_l(l_refs, targets, raw_h, raw_l, inv, l_cat):
    raw_h[...] = jnp.zeros_like(raw_h)
    raw_l[...] = jnp.zeros_like(raw_l)
    for b, ref in enumerate(l_refs):
        for j in range(ref.shape[1]):
            tgt = targets(b, j)

            @pl.when(tgt >= 0)
            def _(ref=ref, j=j, tgt=tgt):
                raw_h[block(tgt), :], raw_l[block(tgt), :] = split(ref[0, j])

    for m in range(0, AR * B, 256):
        hi, lo = scale(raw_h[m : m + 256, :], raw_l[m : m + 256, :], inv)
        l_cat[m : m + 256, 0:W] = hi
        l_cat[m : m + 256, W : 2 * W] = lo


def place_u(u_refs, targets, u_cat):
    for b, ref in enumerate(u_refs):
        for j in range(ref.shape[1]):
            tgt = targets(b, j)

            @pl.when(tgt >= 0)
            def _(ref=ref, j=j, tgt=tgt):
                hi, lo = split(ref[0, j])
                u_cat[0:W, block(tgt)] = hi
                u_cat[W : 2 * W, block(tgt)] = lo


def product(l_cat, u_cat, half):
    rows = slice(half * HALF, (half + 1) * HALF)
    lh, ll = l_cat[rows, 0:W], l_cat[rows, W : 2 * W]
    uh, ul = u_cat[0:W, :], u_cat[W : 2 * W, :]
    return dot(lh, uh) + dot(ll, uh) + dot(lh, ul)


def update_kernel(n_l, n_u, start, first, l_tgt, u_tgt, l_base, u_base, *refs):
    l_refs, u_refs, refs = refs[:n_l], refs[n_l : n_l + n_u], refs[n_l + n_u :]
    inv_ref, _, send_in, keep_in, send, keep, token, raw_h, raw_l, l_cat, u_cat = refs
    step = pl.program_id(0)
    node = start + step

    @pl.when(step == 0)
    def _():
        token[...] = jnp.zeros_like(token)
        if first:
            send[...] = jnp.zeros_like(send)
            keep[...] = keep_in[...]

    rows = lambda b, j: slot_rows(l_tgt, l_base, node, b, j)
    place_l(l_refs, rows, raw_h, raw_l, split(inv_ref[0]), l_cat)
    u_cat[...] = jnp.zeros_like(u_cat)
    place_u(u_refs, lambda b, j: u_tgt[node, u_base[b] + j], u_cat)
    send[...] += product(l_cat, u_cat, 0)
    keep[...] -= product(l_cat, u_cat, 1)


def prepare_kernel(n_l, n_u, start, l_tgt, u_tgt, l_base, u_base, *refs):
    l_refs, u_refs, refs = refs[:n_l], refs[n_l : n_l + n_u], refs[n_l + n_u :]
    inv_ref, _, l_cats, u_cats, token, raw_h, raw_l = refs
    step = pl.program_id(0)
    node = start + step
    token[...] = jnp.zeros_like(token)
    rows = lambda b, j: slot_rows(l_tgt, l_base, node, b, j)
    place_l(l_refs, rows, raw_h, raw_l, split(inv_ref[0]), l_cats.at[step])
    u_cats[step] = jnp.zeros(u_cats.shape[1:], BF16)
    place_u(u_refs, lambda b, j: u_tgt[node, u_base[b] + j], u_cats.at[step])


def finish_kernel(n_l, n_u, start, l_tgt, u_tgt, l_base, u_base, *refs):
    l_refs, u_refs, refs = refs[:n_l], refs[n_l : n_l + n_u], refs[n_l + n_u :]
    inv_ref, _, _, _, _, l_cats, u_cats, send, token = refs
    step = pl.program_id(0)
    node = start + step
    token[...] = jnp.zeros_like(token)
    l_cat, u_cat = l_cats.at[step], u_cats.at[step]
    inv = split(inv_ref[0])
    for b, ref in enumerate(l_refs):
        for j in range(ref.shape[1]):
            tgt = slot_rows(l_tgt, l_base, node, b, j)

            @pl.when(tgt >= 0)
            def _(ref=ref, j=j, tgt=tgt):
                hi, lo = scale(*split(ref[0, j]), inv)
                l_cat[block(tgt), 0:W] = hi
                l_cat[block(tgt), W : 2 * W] = lo

    place_u(u_refs, lambda b, j: u_tgt[node, u_base[b] + j], u_cat)
    send[...] += product(l_cat, u_cat, 0)


def keep_kernel(l_cats, u_cats, _, keep_in, keep):
    step = pl.program_id(0)
    keep[...] -= product(l_cats.at[step], u_cats.at[step], 1)


RAW = pltpu.VMEM((AR * B, W), BF16)
L_CAT = (AR * B, 2 * W)
U_CAT = (2 * W, AC * B)
PARAMS = pltpu.CompilerParams(dimension_semantics=("arbitrary",), vmem_limit_bytes=32 << 20)


def call(kernel, nodes, offsets, tables, l_bufs, u_bufs, u11_inv, token, held, out, fixed, scratch):
    start, stop = nodes

    def per_node(buf, offset):
        return pl.BlockSpec((1,) + buf.shape[1:], lambda s, *_: (offset + s, 0, 0, 0))

    vmem, anywhere = pl.BlockSpec(memory_space=pltpu.VMEM), pl.BlockSpec(memory_space=pl.ANY)
    bufs = [pltpu.with_memory_space_constraint(b, pltpu.HBM) for b in (*l_bufs, *u_bufs)]
    n_in = 6 + len(bufs)
    return pl.pallas_call(
        functools.partial(kernel, len(l_bufs), len(u_bufs), start),
        out_shape=(*out, jax.ShapeDtypeStruct((8, 128), F32)),
        grid_spec=pltpu.PrefetchScalarGridSpec(
            num_scalar_prefetch=4,
            grid=(stop - start,),
            in_specs=[per_node(b, o) for b, o in zip(bufs, offsets)]
            + [pl.BlockSpec((1, W, W), lambda s, *_: (start + s, 0, 0)), anywhere]
            + [vmem] * len(held),
            out_specs=(vmem,) * (len(out) + 1),
            scratch_shapes=scratch,
        ),
        input_output_aliases={n_in + i: i for i in range(len(held))} if fixed else {},
        compiler_params=PARAMS,
    )(*tables, *bufs, u11_inv, token, *held)


def apply_update(nodes, offsets, tables, l_bufs, u_bufs, inv, token, accs, first=False):
    kernel = lambda n_l, n_u, start, *refs: update_kernel(n_l, n_u, start, first, *refs)
    out = [pltpu.VMEM((HALF, AC * B), F32)] * 2
    scratch = [RAW, RAW, pltpu.VMEM(L_CAT, BF16), pltpu.VMEM(U_CAT, BF16)]
    *accs, token = call(
        kernel, nodes, offsets, tables, l_bufs, u_bufs, inv, token, accs, out, not first, scratch
    )
    return token, accs


class Box:
    def __init__(self, value):
        self.value = value


def after(x, boxes):
    if not boxes:
        return x
    x, *values = lax.optimization_barrier((x, *[b.value for b in boxes]))
    for box, value in zip(boxes, values):
        box.value = value
    return x


class Link:
    def __init__(self, axis, wait=()):
        self.axis, self.wait = axis, list(wait)

    def send(self, x, pairs):
        out = Box(lax.ppermute(after(x, self.wait), self.axis, pairs))
        self.wait = [out]
        return out


def up(hop):
    return [(z, z + 1) for z in range(hop - 1, 3)]


def down(hop):
    return [(z, z - 1) for z in range(1, 5 - hop)]


def side(mask):
    return [(r, r ^ mask) for r in range(4)]


def hold(links, box):
    for link in links:
        link.wait.append(box)


class Exchange:
    def __init__(self, links, l_chunk, u_h0, u_h1):
        self.links = links
        self.l, self.h = l_chunk, (u_h0, u_h1)

    def first(self):
        lx, ly, lu, ld = self.links
        self.u1, self.d1 = lu.send(self.l, up(1)), ld.send(self.l, down(1))
        self.x0, self.y1 = lx.send(self.h[0], side(1)), ly.send(self.h[1], side(2))

    def second(self):
        lx, ly, lu, ld = self.links
        self.u2, self.d2 = lu.send(self.u1.value, up(2)), ld.send(self.d1.value, down(2))
        self.x1, self.y0 = lx.send(self.h[1], side(1)), ly.send(self.h[0], side(2))

    def third(self, here):
        lx, ly, lu, ld = self.links
        u3, d3 = lu.send(self.u2.value[here], up(3)), ld.send(self.d2.value[here], down(3))
        f1, f0 = lx.send(self.y1.value[here], side(1)), ly.send(self.x0.value[here], side(2))
        return u3, d3, f0, f1

    def buffers(self, third):
        u3, d3, f0, f1 = third
        l_bufs = [self.l] + [b.value for b in (self.u1, self.d1, self.u2, self.d2, u3, d3)]
        u_bufs = [*self.h] + [b.value for b in (self.x0, self.x1, self.y0, self.y1, f0, f1)]
        return l_bufs, u_bufs


def body(rows, cols, l_panel, l_rows, u_panel, u_cols, u11_inv, ancestor):
    gz, row, col = (lax.axis_index(a) for a in ("gz", "row", "col"))
    l_own, u_own, inv = l_panel[0, :, 0], u_panel[0, :, 0], u11_inv[0]
    nodes, l_slots = l_own.shape[:2]
    u_slots = u_own.shape[1]
    l_tgt = l_rows[0, :, 0]
    l_tgt = jnp.where(l_tgt < 0, -1, (l_tgt + (AR // 2) * (1 - gz)) % AR)
    u_tgt = u_cols[0, :, 0]
    keep = ancestor[0]

    if rows == 4 and cols == 4:
        half = u_slots // 2
        sources = jnp.stack([col, col - 1, col + 1, col - 2, col + 2, col - 3, col + 3])
        l_base = jnp.where((sources >= 0) & (sources < cols), sources * l_slots, -1)
        squares = jnp.stack([row, row, row ^ 1, row ^ 1, row ^ 2, row ^ 2, row ^ 3, row ^ 3])
        u_base = squares * u_slots + half * (jnp.arange(8, dtype=jnp.int32) % 2)
        tables = [t.astype(jnp.int32) for t in (l_tgt, u_tgt, l_base, u_base)]
        links = [Link("row"), Link("row"), Link("col"), Link("col")]
        size, part = nodes // 2, nodes // 4
        chunks = []
        for start in (0, size):
            here = slice(start, start + size)
            chunks.append(Exchange(links, l_own[here], u_own[here, :half], u_own[here, half:]))
        one, two = chunks

        one.first()
        one.second()
        third = one.third(slice(0, size))
        two.first()
        zero = jnp.zeros((8, 128), F32)
        token, accs = apply_update(
            (0, part), [0] * 15, tables, *one.buffers(third), inv, zero, (zero, keep), True
        )
        token = Box(token)
        hold(links, token)
        two.second()
        token, accs = apply_update(
            (part, size), [part] * 15, tables, *one.buffers(third), inv, token.value, accs
        )
        token = Box(token)
        hold(links, token)
        third = two.third(slice(0, size))
        l_bufs, u_bufs = two.buffers(third)
        late = (size, nodes), [0] * 15
        cats = [pltpu.VMEM((size,) + shape, BF16) for shape in (L_CAT, U_CAT)]
        l_cats, u_cats, token = call(
            prepare_kernel, *late, tables, l_bufs[:5], u_bufs[:6], inv, token.value, (), cats, True, [RAW, RAW]
        )
        send, keep = accs
        tables = [l_tgt, u_tgt, l_base[5:], u_base[6:]]
        tables = [t.astype(jnp.int32) for t in tables]
        l_cats, u_cats, send, token = call(
            finish_kernel,
            *late,
            tables,
            l_bufs[5:],
            u_bufs[6:],
            inv,
            token,
            (l_cats, u_cats, send),
            (*cats, pltpu.VMEM((HALF, AC * B), F32)),
            True,
            [],
        )
        vmem = pl.BlockSpec(memory_space=pltpu.VMEM)
        keep = pl.pallas_call(
            keep_kernel,
            grid=(size,),
            out_shape=pltpu.VMEM((HALF, AC * B), F32),
            in_specs=[vmem, vmem, pl.BlockSpec(memory_space=pl.ANY), vmem],
            out_specs=vmem,
            input_output_aliases={3: 0},
            compiler_params=PARAMS,
        )(l_cats, u_cats, token, keep)
    else:
        l_all = lax.all_gather(l_own, "col", axis=1, tiled=True)
        u_all = lax.all_gather(u_own, "row", axis=1, tiled=True)
        base, zero = jnp.zeros((1,), jnp.int32), jnp.zeros((8, 128), F32)
        tables = [t.astype(jnp.int32) for t in (l_tgt, u_tgt, base, base)]
        _, (send, keep) = apply_update(
            (0, nodes), [0, 0], tables, [l_all], [u_all], inv, zero, (zero, keep), True
        )

    other = lax.ppermute(send, "gz", [(0, 1), (1, 0)])
    return (keep - other)[None]


def solution(mesh):
    in_specs = (
        P("gz", None, "row", "col", None, None),
        P("gz", None, "row", None),
        P("gz", None, "col", "row", None, None),
        P("gz", None, "col", None),
        P("gz", None, None, None),
        P("row", "gz", "col"),
    )
    return jax.shard_map(
        functools.partial(body, mesh.shape["row"], mesh.shape["col"]),
        mesh=mesh,
        in_specs=in_specs,
        out_specs=P("row", "gz", "col"),
        check_vma=False,
    )
```

```python
import functools

import jax
import jax.numpy as jnp
from jax import lax
from jax.experimental import pallas as pl
from jax.experimental.pallas import tpu as pltpu
from jax.sharding import PartitionSpec as P

W = 256
B = 128
AR = 8
AC = 16
HALF = AR * B // 2
F32 = jnp.float32
BF16 = jnp.bfloat16


def split(x):
    hi = x.astype(BF16)
    return hi, (x - hi.astype(F32)).astype(BF16)


def dot(a, b):
    return jnp.dot(a, b, preferred_element_type=F32)


def slot_rows(l_tgt, l_base, node, b, j):
    base = l_base[b]
    return jnp.where(base >= 0, l_tgt[node, jnp.maximum(base, 0) + j], -1)


def block(tgt):
    return pl.ds(pl.multiple_of(tgt * B, B), B)


def scale(hi, lo, inv):
    return split(dot(hi, inv[0]) + dot(hi, inv[1]) + dot(lo, inv[0]))


def place_l(l_refs, targets, raw_h, raw_l, inv, l_cat):
    raw_h[...] = jnp.zeros_like(raw_h)
    raw_l[...] = jnp.zeros_like(raw_l)
    for b, ref in enumerate(l_refs):
        for j in range(ref.shape[1]):
            tgt = targets(b, j)

            @pl.when(tgt >= 0)
            def _(ref=ref, j=j, tgt=tgt):
                raw_h[block(tgt), :], raw_l[block(tgt), :] = split(ref[0, j])

    for m in range(0, AR * B, 256):
        hi, lo = scale(raw_h[m : m + 256, :], raw_l[m : m + 256, :], inv)
        l_cat[m : m + 256, 0:W] = hi
        l_cat[m : m + 256, W : 2 * W] = lo


def place_u(u_refs, targets, u_cat):
    for b, ref in enumerate(u_refs):
        for j in range(ref.shape[1]):
            tgt = targets(b, j)

            @pl.when(tgt >= 0)
            def _(ref=ref, j=j, tgt=tgt):
                hi, lo = split(ref[0, j])
                u_cat[0:W, block(tgt)] = hi
                u_cat[W : 2 * W, block(tgt)] = lo


def product(l_cat, u_cat, half):
    rows = slice(half * HALF, (half + 1) * HALF)
    lh, ll = l_cat[rows, 0:W], l_cat[rows, W : 2 * W]
    uh, ul = u_cat[0:W, :], u_cat[W : 2 * W, :]
    return dot(lh, uh) + dot(ll, uh) + dot(lh, ul)


def update_kernel(n_l, n_u, start, first, l_tgt, u_tgt, l_base, u_base, *refs):
    l_refs, u_refs, refs = refs[:n_l], refs[n_l : n_l + n_u], refs[n_l + n_u :]
    inv_ref, _, send_in, keep_in, send, keep, token, raw_h, raw_l, l_cat, u_cat = refs
    step = pl.program_id(0)
    node = start + step

    @pl.when(step == 0)
    def _():
        token[...] = jnp.zeros_like(token)
        if first:
            send[...] = jnp.zeros_like(send)
            keep[...] = keep_in[...]

    rows = lambda b, j: slot_rows(l_tgt, l_base, node, b, j)
    place_l(l_refs, rows, raw_h, raw_l, split(inv_ref[0]), l_cat)
    u_cat[...] = jnp.zeros_like(u_cat)
    place_u(u_refs, lambda b, j: u_tgt[node, u_base[b] + j], u_cat)
    send[...] += product(l_cat, u_cat, 0)
    keep[...] -= product(l_cat, u_cat, 1)


def prepare_kernel(n_l, n_u, start, l_tgt, u_tgt, l_base, u_base, *refs):
    l_refs, u_refs, refs = refs[:n_l], refs[n_l : n_l + n_u], refs[n_l + n_u :]
    inv_ref, _, l_cats, u_cats, token, raw_h, raw_l = refs
    step = pl.program_id(0)
    node = start + step
    token[...] = jnp.zeros_like(token)
    rows = lambda b, j: slot_rows(l_tgt, l_base, node, b, j)
    place_l(l_refs, rows, raw_h, raw_l, split(inv_ref[0]), l_cats.at[step])
    u_cats[step] = jnp.zeros(u_cats.shape[1:], BF16)
    place_u(u_refs, lambda b, j: u_tgt[node, u_base[b] + j], u_cats.at[step])


def finish_kernel(first, halves, n_l, n_u, start, l_tgt, u_tgt, l_base, u_base, *refs):
    l_refs, u_refs, refs = refs[:n_l], refs[n_l : n_l + n_u], refs[n_l + n_u :]
    n = len(halves)
    inv_ref, _, refs = refs[0], refs[1], refs[2:]
    ins, (l_cats, u_cats), accs, token = refs[2 : 2 + n], refs[2 + n : 4 + n], refs[4 + n : 4 + 2 * n], refs[-1]
    step = pl.program_id(0)
    node = start + step
    token[...] = jnp.zeros_like(token)
    if first:

        @pl.when(step == 0)
        def _():
            for half, src, acc in zip(halves, ins, accs):
                acc[...] = src[...] if half else jnp.zeros_like(acc)

    l_cat, u_cat = l_cats.at[step], u_cats.at[step]
    add_l(l_refs, lambda b, j: slot_rows(l_tgt, l_base, node, b, j), inv_ref, l_cat)
    place_u(u_refs, lambda b, j: u_tgt[node, u_base[b] + j], u_cat)
    for half, acc in zip(halves, accs):
        part = product(l_cat, u_cat, half)
        acc[...] = acc[...] - part if half else acc[...] + part


def keep_kernel(l_cats, u_cats, _, keep_in, keep):
    step = pl.program_id(0)
    keep[...] -= product(l_cats.at[step], u_cats.at[step], 1)


def add_l(l_refs, targets, inv_ref, l_cat):
    inv = split(inv_ref[0])
    for b, ref in enumerate(l_refs):
        for j in range(ref.shape[1]):
            tgt = targets(b, j)

            @pl.when(tgt >= 0)
            def _(ref=ref, j=j, tgt=tgt):
                hi, lo = scale(*split(ref[0, j]), inv)
                l_cat[block(tgt), 0:W] = hi
                l_cat[block(tgt), W : 2 * W] = lo


RAW = pltpu.VMEM((AR * B, W), BF16)
L_CAT = (AR * B, 2 * W)
U_CAT = (2 * W, AC * B)
PARAMS = pltpu.CompilerParams(dimension_semantics=("arbitrary",), vmem_limit_bytes=20 << 20)


def call(kernel, nodes, offsets, tables, l_bufs, u_bufs, u11_inv, token, held, out, aliases, scratch, pin=True):
    start, stop = nodes

    def per_node(buf, offset):
        return pl.BlockSpec((1,) + buf.shape[1:], lambda s, *_: (offset + s, 0, 0, 0))

    vmem, anywhere = pl.BlockSpec(memory_space=pltpu.VMEM), pl.BlockSpec(memory_space=pl.ANY)
    bufs = [*l_bufs, *u_bufs]
    if pin:
        bufs = [pltpu.with_memory_space_constraint(b, pltpu.HBM) for b in bufs]
    n_in = 6 + len(bufs)
    return pl.pallas_call(
        functools.partial(kernel, len(l_bufs), len(u_bufs), start),
        out_shape=(*out, jax.ShapeDtypeStruct((8, 128), F32)),
        grid_spec=pltpu.PrefetchScalarGridSpec(
            num_scalar_prefetch=4,
            grid=(stop - start,),
            in_specs=[per_node(b, o) for b, o in zip(bufs, offsets)]
            + [pl.BlockSpec((1, W, W), lambda s, *_: (start + s, 0, 0)), anywhere]
            + [vmem] * len(held),
            out_specs=(vmem,) * (len(out) + 1),
            scratch_shapes=scratch,
        ),
        input_output_aliases={n_in + i: o for i, o in aliases.items()},
        compiler_params=PARAMS,
    )(*tables, *bufs, u11_inv, token, *held)


ACC = pltpu.VMEM((HALF, AC * B), F32)


def apply_update(nodes, tables, l_bufs, u_bufs, inv, token, keep):
    kernel = lambda n_l, n_u, start, *refs: update_kernel(n_l, n_u, start, True, *refs)
    scratch = [RAW, RAW, pltpu.VMEM(L_CAT, BF16), pltpu.VMEM(U_CAT, BF16)]
    offsets = [0] * (len(l_bufs) + len(u_bufs))
    send, keep, _ = call(
        kernel, nodes, offsets, tables, l_bufs, u_bufs, inv, token, (token, keep), [ACC] * 2, {}, scratch
    )
    return send, keep


class Box:
    def __init__(self, value):
        self.value = value


def after(x, boxes):
    if not boxes:
        return x
    x, *values = lax.optimization_barrier((x, *[b.value for b in boxes]))
    for box, value in zip(boxes, values):
        box.value = value
    return x


class Link:
    def __init__(self, axis, wait=()):
        self.axis, self.wait = axis, list(wait)

    def send(self, x, pairs):
        out = Box(lax.ppermute(after(x, self.wait), self.axis, pairs))
        self.wait = [out]
        return out


def up(hop):
    return [(z, z + 1) for z in range(hop - 1, 3)]


def down(hop):
    return [(z, z - 1) for z in range(1, 5 - hop)]


def side(mask):
    return [(r, r ^ mask) for r in range(4)]


def hold(links, box):
    for link in links:
        link.wait.append(box)


class Exchange:
    def __init__(self, links, l_chunk, u_h0, u_h1):
        self.links = links
        self.l, self.h = l_chunk, (u_h0, u_h1)

    def first(self):
        lx, ly, lu, ld = self.links
        self.u1, self.d1 = lu.send(self.l, up(1)), ld.send(self.l, down(1))
        self.x0, self.y1 = lx.send(self.h[0], side(1)), ly.send(self.h[1], side(2))

    def second(self):
        lx, ly, lu, ld = self.links
        self.u2, self.d2 = lu.send(self.u1.value, up(2)), ld.send(self.d1.value, down(2))
        self.x1, self.y0 = lx.send(self.h[1], side(1)), ly.send(self.h[0], side(2))

    def third(self, here):
        lx, ly, lu, ld = self.links
        u3, d3 = lu.send(self.u2.value[here], up(3)), ld.send(self.d2.value[here], down(3))
        f1, f0 = lx.send(self.y1.value[here], side(1)), ly.send(self.x0.value[here], side(2))
        return u3, d3, f0, f1

    def buffers(self, third):
        names = ("u1", "d1", "u2", "d2", "x0", "x1", "y0", "y1")
        v = {n: getattr(self, n).value if hasattr(self, n) else None for n in names}
        u3, d3, f0, f1 = (b.value for b in third)
        l_bufs = [self.l, v["u1"], v["d1"], v["u2"], v["d2"], u3, d3]
        u_bufs = [*self.h, v["x0"], v["y1"], v["x1"], v["y0"], f0, f1]
        return l_bufs, u_bufs


def body(rows, cols, l_panel, l_rows, u_panel, u_cols, u11_inv, ancestor):
    gz, row, col = (lax.axis_index(a) for a in ("gz", "row", "col"))
    l_own, u_own, inv = l_panel[0, :, 0], u_panel[0, :, 0], u11_inv[0]
    nodes, l_slots = l_own.shape[:2]
    u_slots = u_own.shape[1]
    l_tgt = l_rows[0, :, 0]
    l_tgt = jnp.where(l_tgt < 0, -1, (l_tgt + (AR // 2) * (1 - gz)) % AR)
    u_tgt = u_cols[0, :, 0]
    keep = ancestor[0]

    if rows == 4 and cols == 4:
        half = u_slots // 2
        sources = jnp.stack([col, col - 1, col + 1, col - 2, col + 2, col - 3, col + 3])
        l_base = jnp.where((sources >= 0) & (sources < cols), sources * l_slots, -1)
        squares = jnp.stack([row, row, row ^ 1, row ^ 2, row ^ 1, row ^ 2, row ^ 3, row ^ 3])
        u_base = squares * u_slots + half * jnp.array([0, 1, 0, 1, 1, 0, 0, 1], jnp.int32)
        links = [Link("row"), Link("row"), Link("col"), Link("col")]
        size = 5
        chunks = []
        for here in (slice(0, size), slice(size, nodes)):
            chunks.append(Exchange(links, l_own[here], u_own[here, :half], u_own[here, half:]))
        one, two = chunks
        one.first()
        one.second()
        third = one.third(slice(0, size))
        zero = jnp.zeros((8, 128), F32)

        def run(kernel, chunk, third, here, ls, us, token, held, out, aliases, scratch=(), pin=True):
            l_bufs, u_bufs = chunk.buffers(third)
            tables = [t.astype(jnp.int32) for t in (l_tgt, u_tgt, l_base[ls], u_base[us])]
            l_bufs, u_bufs = l_bufs[ls], u_bufs[us]
            offsets = [here[0] - (0 if chunk is one else size)] * (len(l_bufs) + len(u_bufs))
            return call(
                kernel, here, offsets, tables, l_bufs, u_bufs, inv, token, held, out, aliases, list(scratch), pin
            )

        def cats(count):
            return [pltpu.VMEM((count,) + shape, BF16) for shape in (L_CAT, U_CAT)]

        early, late = (slice(0, 5), slice(0, 6)), (slice(5, 7), slice(6, 8))
        parts = ((0, 3), (3, size))
        held = []
        token = zero
        for here in parts:
            *cat, token = run(
                prepare_kernel, one, third, here, *early, token, (), cats(here[1] - here[0]), {}, (RAW, RAW)
            )
            held.append(cat)
        token = Box(token)
        hold(links, token)
        accs, first = (zero, keep), True
        for stage, here, cat in zip((two.first, two.second), parts, held):
            stage()
            *_, send, keep, token = run(
                functools.partial(finish_kernel, first, (0, 1)),
                one,
                third,
                here,
                *late,
                token.value,
                (*cat, *accs),
                [*cats(here[1] - here[0]), ACC, ACC],
                {0: 0, 1: 1} if first else {0: 0, 1: 1, 2: 2, 3: 3},
            )
            accs, first, token = (send, keep), False, Box(token)
            hold(links, token)
        last = two.third(slice(0, nodes - size))
        here = (size, nodes)
        *cat, token = run(
            prepare_kernel, two, last, here, *early, token.value, (), cats(nodes - size), {}, (RAW, RAW)
        )
        *cat, send, token = run(
            functools.partial(finish_kernel, False, (0,)),
            two,
            last,
            here,
            *late,
            token,
            (*cat, send),
            [*cats(nodes - size), ACC],
            {0: 0, 1: 1, 2: 2},
            pin=False,
        )
        vmem = pl.BlockSpec(memory_space=pltpu.VMEM)
        keep = pl.pallas_call(
            keep_kernel,
            grid=(nodes - size,),
            out_shape=ACC,
            in_specs=[vmem, vmem, pl.BlockSpec(memory_space=pl.ANY), vmem],
            out_specs=vmem,
            input_output_aliases={3: 0},
            compiler_params=PARAMS,
        )(*cat, token, keep)
    else:
        l_all = lax.all_gather(l_own, "col", axis=1, tiled=True)
        u_all = lax.all_gather(u_own, "row", axis=1, tiled=True)
        base, zero = jnp.zeros((1,), jnp.int32), jnp.zeros((8, 128), F32)
        tables = [t.astype(jnp.int32) for t in (l_tgt, u_tgt, base, base)]
        send, keep = apply_update((0, nodes), tables, [l_all], [u_all], inv, zero, keep)

    other = lax.ppermute(send, "gz", [(0, 1), (1, 0)])
    return (keep - other)[None]


def solution(mesh):
    in_specs = (
        P("gz", None, "row", "col", None, None),
        P("gz", None, "row", None),
        P("gz", None, "col", "row", None, None),
        P("gz", None, "col", None),
        P("gz", None, None, None),
        P("row", "gz", "col"),
    )
    return jax.shard_map(
        functools.partial(body, mesh.shape["row"], mesh.shape["col"]),
        mesh=mesh,
        in_specs=in_specs,
        out_specs=P("row", "gz", "col"),
        check_vma=False,
    )
```

```python
import functools

import jax
import jax.numpy as jnp
from jax import lax
from jax.experimental import pallas as pl
from jax.experimental.pallas import tpu as pltpu
from jax.sharding import PartitionSpec as P

W = 256
B = 128
AR = 8
AC = 16
HALF = AR * B // 2
F32 = jnp.float32
BF16 = jnp.bfloat16


def split(x):
    hi = x.astype(BF16)
    return hi, (x - hi.astype(F32)).astype(BF16)


def dot(a, b):
    return jnp.dot(a, b, preferred_element_type=F32)


def slot_rows(l_tgt, l_base, node, b, j):
    base = l_base[b]
    return jnp.where(base >= 0, l_tgt[node, jnp.maximum(base, 0) + j], -1)


def block(tgt):
    return pl.ds(pl.multiple_of(tgt * B, B), B)


def scale(hi, lo, inv):
    return split(dot(hi, inv[0]) + dot(hi, inv[1]) + dot(lo, inv[0]))


def place_l(l_refs, targets, raw_h, raw_l, inv, l_cat):
    raw_h[...] = jnp.zeros_like(raw_h)
    raw_l[...] = jnp.zeros_like(raw_l)
    for b, ref in enumerate(l_refs):
        for j in range(ref.shape[1]):
            tgt = targets(b, j)

            @pl.when(tgt >= 0)
            def _(ref=ref, j=j, tgt=tgt):
                raw_h[block(tgt), :], raw_l[block(tgt), :] = split(ref[0, j])

    for m in range(0, AR * B, 256):
        hi, lo = scale(raw_h[m : m + 256, :], raw_l[m : m + 256, :], inv)
        l_cat[m : m + 256, 0:W] = hi
        l_cat[m : m + 256, W : 2 * W] = lo


def place_u(u_refs, targets, u_cat):
    for b, ref in enumerate(u_refs):
        for j in range(ref.shape[1]):
            tgt = targets(b, j)

            @pl.when(tgt >= 0)
            def _(ref=ref, j=j, tgt=tgt):
                hi, lo = split(ref[0, j])
                u_cat[0:W, block(tgt)] = hi
                u_cat[W : 2 * W, block(tgt)] = lo


def product(l_cat, u_cat, half):
    rows = slice(half * HALF, (half + 1) * HALF)
    lh, ll = l_cat[rows, 0:W], l_cat[rows, W : 2 * W]
    uh, ul = u_cat[0:W, :], u_cat[W : 2 * W, :]
    return dot(lh, uh) + dot(ll, uh) + dot(lh, ul)


def update_kernel(n_l, n_u, start, first, l_tgt, u_tgt, l_base, u_base, *refs):
    l_refs, u_refs, refs = refs[:n_l], refs[n_l : n_l + n_u], refs[n_l + n_u :]
    inv_ref, _, send_in, keep_in, send, keep, token, raw_h, raw_l, l_cat, u_cat = refs
    step = pl.program_id(0)
    node = start + step

    @pl.when(step == 0)
    def _():
        token[...] = jnp.zeros_like(token)
        if first:
            send[...] = jnp.zeros_like(send)
            keep[...] = keep_in[...]

    rows = lambda b, j: slot_rows(l_tgt, l_base, node, b, j)
    place_l(l_refs, rows, raw_h, raw_l, split(inv_ref[0]), l_cat)
    u_cat[...] = jnp.zeros_like(u_cat)
    place_u(u_refs, lambda b, j: u_tgt[node, u_base[b] + j], u_cat)
    send[...] += product(l_cat, u_cat, 0)
    keep[...] -= product(l_cat, u_cat, 1)


def prepare_kernel(n_l, n_u, start, l_tgt, u_tgt, l_base, u_base, *refs):
    l_refs, u_refs, refs = refs[:n_l], refs[n_l : n_l + n_u], refs[n_l + n_u :]
    inv_ref, _, l_cats, u_cats, token, raw_h, raw_l = refs
    step = pl.program_id(0)
    node = start + step
    token[...] = jnp.zeros_like(token)
    rows = lambda b, j: slot_rows(l_tgt, l_base, node, b, j)
    place_l(l_refs, rows, raw_h, raw_l, split(inv_ref[0]), l_cats.at[step])
    u_cats[step] = jnp.zeros(u_cats.shape[1:], BF16)
    place_u(u_refs, lambda b, j: u_tgt[node, u_base[b] + j], u_cats.at[step])


def finish_kernel(first, halves, n_l, n_u, start, l_tgt, u_tgt, l_base, u_base, *refs):
    l_refs, u_refs, refs = refs[:n_l], refs[n_l : n_l + n_u], refs[n_l + n_u :]
    n = len(halves)
    inv_ref, _, refs = refs[0], refs[1], refs[2:]
    ins, (l_cats, u_cats), accs, token = refs[2 : 2 + n], refs[2 + n : 4 + n], refs[4 + n : 4 + 2 * n], refs[-1]
    step = pl.program_id(0)
    node = start + step
    token[...] = jnp.zeros_like(token)
    if first:

        @pl.when(step == 0)
        def _():
            for half, src, acc in zip(halves, ins, accs):
                acc[...] = src[...] if half else jnp.zeros_like(acc)

    l_cat, u_cat = l_cats.at[step], u_cats.at[step]
    add_l(l_refs, lambda b, j: slot_rows(l_tgt, l_base, node, b, j), inv_ref, l_cat)
    place_u(u_refs, lambda b, j: u_tgt[node, u_base[b] + j], u_cat)
    for half, acc in zip(halves, accs):
        part = product(l_cat, u_cat, half)
        acc[...] = acc[...] - part if half else acc[...] + part


def keep_kernel(l_cats, u_cats, _, keep_in, keep):
    step = pl.program_id(0)
    keep[...] -= product(l_cats.at[step], u_cats.at[step], 1)


def add_l(l_refs, targets, inv_ref, l_cat):
    inv = split(inv_ref[0])
    for b, ref in enumerate(l_refs):
        for j in range(ref.shape[1]):
            tgt = targets(b, j)

            @pl.when(tgt >= 0)
            def _(ref=ref, j=j, tgt=tgt):
                hi, lo = scale(*split(ref[0, j]), inv)
                l_cat[block(tgt), 0:W] = hi
                l_cat[block(tgt), W : 2 * W] = lo


RAW = pltpu.VMEM((AR * B, W), BF16)
L_CAT = (AR * B, 2 * W)
U_CAT = (2 * W, AC * B)
PARAMS = pltpu.CompilerParams(dimension_semantics=("arbitrary",), vmem_limit_bytes=20 << 20)


def call(kernel, nodes, offsets, tables, l_bufs, u_bufs, u11_inv, token, held, out, aliases, scratch, pin=True):
    start, stop = nodes

    def per_node(buf, offset):
        return pl.BlockSpec((1,) + buf.shape[1:], lambda s, *_: (offset + s, 0, 0, 0))

    vmem, anywhere = pl.BlockSpec(memory_space=pltpu.VMEM), pl.BlockSpec(memory_space=pl.ANY)
    bufs = [*l_bufs, *u_bufs]
    if pin:
        bufs = [pltpu.with_memory_space_constraint(b, pltpu.HBM) for b in bufs]
    n_in = 6 + len(bufs)
    return pl.pallas_call(
        functools.partial(kernel, len(l_bufs), len(u_bufs), start),
        out_shape=(*out, jax.ShapeDtypeStruct((8, 128), F32)),
        grid_spec=pltpu.PrefetchScalarGridSpec(
            num_scalar_prefetch=4,
            grid=(stop - start,),
            in_specs=[per_node(b, o) for b, o in zip(bufs, offsets)]
            + [pl.BlockSpec((1, W, W), lambda s, *_: (start + s, 0, 0)), anywhere]
            + [vmem] * len(held),
            out_specs=(vmem,) * (len(out) + 1),
            scratch_shapes=scratch,
        ),
        input_output_aliases={n_in + i: o for i, o in aliases.items()},
        compiler_params=PARAMS,
    )(*tables, *bufs, u11_inv, token, *held)


ACC = pltpu.VMEM((HALF, AC * B), F32)


def apply_update(nodes, tables, l_bufs, u_bufs, inv, token, keep):
    kernel = lambda n_l, n_u, start, *refs: update_kernel(n_l, n_u, start, True, *refs)
    scratch = [RAW, RAW, pltpu.VMEM(L_CAT, BF16), pltpu.VMEM(U_CAT, BF16)]
    offsets = [0] * (len(l_bufs) + len(u_bufs))
    send, keep, _ = call(
        kernel, nodes, offsets, tables, l_bufs, u_bufs, inv, token, (token, keep), [ACC] * 2, {}, scratch
    )
    return send, keep


class Box:
    def __init__(self, value):
        self.value = value


def after(x, boxes):
    if not boxes:
        return x
    x, *values = lax.optimization_barrier((x, *[b.value for b in boxes]))
    for box, value in zip(boxes, values):
        box.value = value
    return x


class Link:
    def __init__(self, axis, wait=()):
        self.axis, self.wait = axis, list(wait)

    def send(self, x, pairs):
        out = Box(lax.ppermute(after(x, self.wait), self.axis, pairs))
        self.wait = [out]
        return out


def up(hop):
    return [(z, z + 1) for z in range(hop - 1, 3)]


def down(hop):
    return [(z, z - 1) for z in range(1, 5 - hop)]


def side(mask):
    return [(r, r ^ mask) for r in range(4)]


def hold(links, box):
    for link in links:
        link.wait.append(box)


class Exchange:
    def __init__(self, links, l_chunk, u_h0, u_h1):
        self.links = links
        self.l, self.h = l_chunk, (u_h0, u_h1)

    def first(self):
        lx, ly, lu, ld = self.links
        self.x0, self.y1 = lx.send(self.h[0], side(1)), ly.send(self.h[1], side(2))
        self.u1, self.d1 = lu.send(self.l, up(1)), ld.send(self.l, down(1))

    def second(self):
        lx, ly, lu, ld = self.links
        self.x1, self.y0 = lx.send(self.h[1], side(1)), ly.send(self.h[0], side(2))
        self.u2, self.d2 = lu.send(self.u1.value, up(2)), ld.send(self.d1.value, down(2))

    def third(self, here):
        lx, ly, lu, ld = self.links
        f1, f0 = lx.send(self.y1.value[here], side(1)), ly.send(self.x0.value[here], side(2))
        u3, d3 = lu.send(self.u2.value[here], up(3)), ld.send(self.d2.value[here], down(3))
        return u3, d3, f0, f1

    def buffers(self, third):
        names = ("u1", "d1", "u2", "d2", "x0", "x1", "y0", "y1")
        v = {n: getattr(self, n).value if hasattr(self, n) else None for n in names}
        u3, d3, f0, f1 = (b.value for b in third)
        l_bufs = [self.l, v["u1"], v["d1"], v["u2"], v["d2"], u3, d3]
        u_bufs = [*self.h, v["x0"], v["y1"], v["x1"], v["y0"], f0, f1]
        return l_bufs, u_bufs


def body(rows, cols, l_panel, l_rows, u_panel, u_cols, u11_inv, ancestor):
    gz, row, col = (lax.axis_index(a) for a in ("gz", "row", "col"))
    l_own, u_own, inv = l_panel[0, :, 0], u_panel[0, :, 0], u11_inv[0]
    nodes, l_slots = l_own.shape[:2]
    u_slots = u_own.shape[1]
    l_tgt = l_rows[0, :, 0]
    l_tgt = jnp.where(l_tgt < 0, -1, (l_tgt + (AR // 2) * (1 - gz)) % AR)
    u_tgt = u_cols[0, :, 0]
    keep = ancestor[0]

    if rows == 4 and cols == 4:
        half = u_slots // 2
        sources = jnp.stack([col, col - 1, col + 1, col - 2, col + 2, col - 3, col + 3])
        l_base = jnp.where((sources >= 0) & (sources < cols), sources * l_slots, -1)
        squares = jnp.stack([row, row, row ^ 1, row ^ 2, row ^ 1, row ^ 2, row ^ 3, row ^ 3])
        u_base = squares * u_slots + half * jnp.array([0, 1, 0, 1, 1, 0, 0, 1], jnp.int32)
        links = [Link("row"), Link("row"), Link("col"), Link("col")]
        size = 5
        chunks = []
        for here in (slice(0, size), slice(size, nodes)):
            chunks.append(Exchange(links, l_own[here], u_own[here, :half], u_own[here, half:]))
        one, two = chunks
        one.first()
        one.second()
        third = one.third(slice(0, size))
        zero = jnp.zeros((8, 128), F32)

        def run(kernel, chunk, third, here, ls, us, token, held, out, aliases, scratch=(), pin=True):
            l_bufs, u_bufs = chunk.buffers(third)
            tables = [t.astype(jnp.int32) for t in (l_tgt, u_tgt, l_base[ls], u_base[us])]
            l_bufs, u_bufs = l_bufs[ls], u_bufs[us]
            offsets = [here[0] - (0 if chunk is one else size)] * (len(l_bufs) + len(u_bufs))
            return call(
                kernel, here, offsets, tables, l_bufs, u_bufs, inv, token, held, out, aliases, list(scratch), pin
            )

        def cats(count):
            return [pltpu.VMEM((count,) + shape, BF16) for shape in (L_CAT, U_CAT)]

        early, late = (slice(0, 5), slice(0, 6)), (slice(5, 7), slice(6, 8))
        parts = ((0, 3), (3, size))
        held = []
        token = zero
        for here in parts:
            *cat, token = run(
                prepare_kernel, one, third, here, *early, token, (), cats(here[1] - here[0]), {}, (RAW, RAW)
            )
            held.append(cat)
        token = Box(token)
        hold(links, token)
        accs, first = (zero, keep), True
        for stage, here, cat in zip((two.first, two.second), parts, held):
            stage()
            *_, send, keep, token = run(
                functools.partial(finish_kernel, first, (0, 1)),
                one,
                third,
                here,
                *late,
                token.value,
                (*cat, *accs),
                [*cats(here[1] - here[0]), ACC, ACC],
                {0: 0, 1: 1} if first else {0: 0, 1: 1, 2: 2, 3: 3},
            )
            accs, first, token = (send, keep), False, Box(token)
            hold(links, token)
        last = two.third(slice(0, nodes - size))
        here = (size, nodes)
        *cat, token = run(
            prepare_kernel, two, last, here, *early, token.value, (), cats(nodes - size), {}, (RAW, RAW)
        )
        *cat, send, token = run(
            functools.partial(finish_kernel, False, (0,)),
            two,
            last,
            here,
            *late,
            token,
            (*cat, send),
            [*cats(nodes - size), ACC],
            {0: 0, 1: 1, 2: 2},
            pin=False,
        )
        vmem = pl.BlockSpec(memory_space=pltpu.VMEM)
        keep = pl.pallas_call(
            keep_kernel,
            grid=(nodes - size,),
            out_shape=ACC,
            in_specs=[vmem, vmem, pl.BlockSpec(memory_space=pl.ANY), vmem],
            out_specs=vmem,
            input_output_aliases={3: 0},
            compiler_params=PARAMS,
        )(*cat, token, keep)
    else:
        l_all = lax.all_gather(l_own, "col", axis=1, tiled=True)
        u_all = lax.all_gather(u_own, "row", axis=1, tiled=True)
        base, zero = jnp.zeros((1,), jnp.int32), jnp.zeros((8, 128), F32)
        tables = [t.astype(jnp.int32) for t in (l_tgt, u_tgt, base, base)]
        send, keep = apply_update((0, nodes), tables, [l_all], [u_all], inv, zero, keep)

    other = lax.ppermute(send, "gz", [(0, 1), (1, 0)])
    return (keep - other)[None]


def solution(mesh):
    in_specs = (
        P("gz", None, "row", "col", None, None),
        P("gz", None, "row", None),
        P("gz", None, "col", "row", None, None),
        P("gz", None, "col", None),
        P("gz", None, None, None),
        P("row", "gz", "col"),
    )
    return jax.shard_map(
        functools.partial(body, mesh.shape["row"], mesh.shape["col"]),
        mesh=mesh,
        in_specs=in_specs,
        out_specs=P("row", "gz", "col"),
        check_vma=False,
    )
```

```python
import functools

import jax
import jax.numpy as jnp
from jax import lax
from jax.experimental import pallas as pl
from jax.experimental.pallas import tpu as pltpu
from jax.sharding import PartitionSpec as P

W = 256
B = 128
AR = 8
AC = 16
HALF = AR * B // 2
F32 = jnp.float32
BF16 = jnp.bfloat16


def split(x):
    hi = x.astype(BF16)
    return hi, (x - hi.astype(F32)).astype(BF16)


def dot(a, b):
    return jnp.dot(a, b, preferred_element_type=F32)


def slot_rows(l_tgt, l_base, node, b, j):
    base = l_base[b]
    return jnp.where(base >= 0, l_tgt[node, jnp.maximum(base, 0) + j], -1)


def block(tgt):
    return pl.ds(pl.multiple_of(tgt * B, B), B)


def scale(hi, lo, inv):
    return split(dot(hi, inv[0]) + dot(hi, inv[1]) + dot(lo, inv[0]))


def place_l(l_refs, targets, raw_h, raw_l, inv, l_cat):
    raw_h[...] = jnp.zeros_like(raw_h)
    raw_l[...] = jnp.zeros_like(raw_l)
    for b, ref in enumerate(l_refs):
        for j in range(ref.shape[1]):
            tgt = targets(b, j)

            @pl.when(tgt >= 0)
            def _(ref=ref, j=j, tgt=tgt):
                raw_h[block(tgt), :], raw_l[block(tgt), :] = split(ref[0, j])

    for m in range(0, AR * B, 256):
        hi, lo = scale(raw_h[m : m + 256, :], raw_l[m : m + 256, :], inv)
        l_cat[m : m + 256, 0:W] = hi
        l_cat[m : m + 256, W : 2 * W] = lo


def place_u(u_refs, targets, u_cat):
    for b, ref in enumerate(u_refs):
        for j in range(ref.shape[1]):
            tgt = targets(b, j)

            @pl.when(tgt >= 0)
            def _(ref=ref, j=j, tgt=tgt):
                hi, lo = split(ref[0, j])
                u_cat[0:W, block(tgt)] = hi
                u_cat[W : 2 * W, block(tgt)] = lo


def product(l_cat, u_cat, half):
    rows = slice(half * HALF, (half + 1) * HALF)
    lh, ll = l_cat[rows, 0:W], l_cat[rows, W : 2 * W]
    uh, ul = u_cat[0:W, :], u_cat[W : 2 * W, :]
    return dot(lh, uh) + dot(ll, uh) + dot(lh, ul)


def update_kernel(n_l, n_u, start, first, l_tgt, u_tgt, l_base, u_base, *refs):
    l_refs, u_refs, refs = refs[:n_l], refs[n_l : n_l + n_u], refs[n_l + n_u :]
    inv_ref, _, send_in, keep_in, send, keep, token, raw_h, raw_l, l_cat, u_cat = refs
    step = pl.program_id(0)
    node = start + step

    @pl.when(step == 0)
    def _():
        token[...] = jnp.zeros_like(token)
        if first:
            send[...] = jnp.zeros_like(send)
            keep[...] = keep_in[...]

    rows = lambda b, j: slot_rows(l_tgt, l_base, node, b, j)
    place_l(l_refs, rows, raw_h, raw_l, split(inv_ref[0]), l_cat)
    u_cat[...] = jnp.zeros_like(u_cat)
    place_u(u_refs, lambda b, j: u_tgt[node, u_base[b] + j], u_cat)
    send[...] += product(l_cat, u_cat, 0)
    keep[...] -= product(l_cat, u_cat, 1)


def prepare_kernel(n_l, n_u, start, l_tgt, u_tgt, l_base, u_base, *refs):
    l_refs, u_refs, refs = refs[:n_l], refs[n_l : n_l + n_u], refs[n_l + n_u :]
    inv_ref, _, l_cats, u_cats, token, raw_h, raw_l = refs
    step = pl.program_id(0)
    node = start + step
    token[...] = jnp.zeros_like(token)
    rows = lambda b, j: slot_rows(l_tgt, l_base, node, b, j)
    place_l(l_refs, rows, raw_h, raw_l, split(inv_ref[0]), l_cats.at[step])
    u_cats[step] = jnp.zeros(u_cats.shape[1:], BF16)
    place_u(u_refs, lambda b, j: u_tgt[node, u_base[b] + j], u_cats.at[step])


def finish_kernel(first, halves, n_l, n_u, start, l_tgt, u_tgt, l_base, u_base, *refs):
    l_refs, u_refs, refs = refs[:n_l], refs[n_l : n_l + n_u], refs[n_l + n_u :]
    n = len(halves)
    inv_ref, _, refs = refs[0], refs[1], refs[2:]
    ins, (l_cats, u_cats), accs, token = refs[2 : 2 + n], refs[2 + n : 4 + n], refs[4 + n : 4 + 2 * n], refs[-1]
    step = pl.program_id(0)
    node = start + step
    token[...] = jnp.zeros_like(token)
    if first:

        @pl.when(step == 0)
        def _():
            for half, src, acc in zip(halves, ins, accs):
                acc[...] = src[...] if half else jnp.zeros_like(acc)

    l_cat, u_cat = l_cats.at[step], u_cats.at[step]
    add_l(l_refs, lambda b, j: slot_rows(l_tgt, l_base, node, b, j), inv_ref, l_cat)
    place_u(u_refs, lambda b, j: u_tgt[node, u_base[b] + j], u_cat)
    for half, acc in zip(halves, accs):
        part = product(l_cat, u_cat, half)
        acc[...] = acc[...] - part if half else acc[...] + part


def keep_kernel(l_cats, u_cats, _, keep_in, keep):
    step = pl.program_id(0)
    keep[...] -= product(l_cats.at[step], u_cats.at[step], 1)


def add_l(l_refs, targets, inv_ref, l_cat):
    inv = split(inv_ref[0])
    for b, ref in enumerate(l_refs):
        for j in range(ref.shape[1]):
            tgt = targets(b, j)

            @pl.when(tgt >= 0)
            def _(ref=ref, j=j, tgt=tgt):
                hi, lo = scale(*split(ref[0, j]), inv)
                l_cat[block(tgt), 0:W] = hi
                l_cat[block(tgt), W : 2 * W] = lo


RAW = pltpu.VMEM((AR * B, W), BF16)
L_CAT = (AR * B, 2 * W)
U_CAT = (2 * W, AC * B)
PARAMS = pltpu.CompilerParams(dimension_semantics=("arbitrary",), vmem_limit_bytes=20 << 20)


def call(kernel, nodes, offsets, tables, l_bufs, u_bufs, u11_inv, token, held, out, aliases, scratch, pin=True):
    start, stop = nodes

    def per_node(buf, offset):
        return pl.BlockSpec((1,) + buf.shape[1:], lambda s, *_: (offset + s, 0, 0, 0))

    vmem, anywhere = pl.BlockSpec(memory_space=pltpu.VMEM), pl.BlockSpec(memory_space=pl.ANY)
    bufs = [*l_bufs, *u_bufs]
    if pin:
        bufs = [pltpu.with_memory_space_constraint(b, pltpu.HBM) for b in bufs]
    n_in = 6 + len(bufs)
    return pl.pallas_call(
        functools.partial(kernel, len(l_bufs), len(u_bufs), start),
        out_shape=(*out, jax.ShapeDtypeStruct((8, 128), F32)),
        grid_spec=pltpu.PrefetchScalarGridSpec(
            num_scalar_prefetch=4,
            grid=(stop - start,),
            in_specs=[per_node(b, o) for b, o in zip(bufs, offsets)]
            + [pl.BlockSpec((1, W, W), lambda s, *_: (start + s, 0, 0)), anywhere]
            + [vmem] * len(held),
            out_specs=(vmem,) * (len(out) + 1),
            scratch_shapes=scratch,
        ),
        input_output_aliases={n_in + i: o for i, o in aliases.items()},
        compiler_params=PARAMS,
    )(*tables, *bufs, u11_inv, token, *held)


ACC = pltpu.VMEM((HALF, AC * B), F32)


def apply_update(nodes, tables, l_bufs, u_bufs, inv, token, keep):
    kernel = lambda n_l, n_u, start, *refs: update_kernel(n_l, n_u, start, True, *refs)
    scratch = [RAW, RAW, pltpu.VMEM(L_CAT, BF16), pltpu.VMEM(U_CAT, BF16)]
    offsets = [0] * (len(l_bufs) + len(u_bufs))
    send, keep, _ = call(
        kernel, nodes, offsets, tables, l_bufs, u_bufs, inv, token, (token, keep), [ACC] * 2, {}, scratch
    )
    return send, keep


class Box:
    def __init__(self, value):
        self.value = value


def after(x, boxes):
    if not boxes:
        return x
    x, *values = lax.optimization_barrier((x, *[b.value for b in boxes]))
    for box, value in zip(boxes, values):
        box.value = value
    return x


class Link:
    def __init__(self, axis, wait=()):
        self.axis, self.wait = axis, list(wait)

    def send(self, x, pairs):
        out = Box(lax.ppermute(after(x, self.wait), self.axis, pairs))
        self.wait = [out]
        return out


def up(hop):
    return [(z, z + 1) for z in range(hop - 1, 3)]


def down(hop):
    return [(z, z - 1) for z in range(1, 5 - hop)]


def side(mask):
    return [(r, r ^ mask) for r in range(4)]


def hold(links, box):
    for link in links:
        link.wait.append(box)


class Exchange:
    def __init__(self, links, l_chunk, u_h0, u_h1):
        self.links = links
        self.l, self.h = l_chunk, (u_h0, u_h1)

    def first(self):
        lx, ly, lu, ld = self.links
        self.x0, self.y1 = lx.send(self.h[0], side(1)), ly.send(self.h[1], side(2))
        self.d1, self.u1 = ld.send(self.l, down(1)), lu.send(self.l, up(1))

    def second(self):
        lx, ly, lu, ld = self.links
        self.x1, self.y0 = lx.send(self.h[1], side(1)), ly.send(self.h[0], side(2))
        self.d2, self.u2 = ld.send(self.d1.value, down(2)), lu.send(self.u1.value, up(2))

    def third(self, here):
        lx, ly, lu, ld = self.links
        f1, f0 = lx.send(self.y1.value[here], side(1)), ly.send(self.x0.value[here], side(2))
        d3, u3 = ld.send(self.d2.value[here], down(3)), lu.send(self.u2.value[here], up(3))
        return u3, d3, f0, f1

    def buffers(self, third):
        names = ("u1", "d1", "u2", "d2", "x0", "x1", "y0", "y1")
        v = {n: getattr(self, n).value if hasattr(self, n) else None for n in names}
        u3, d3, f0, f1 = (b.value for b in third)
        l_bufs = [self.l, v["u1"], v["d1"], v["u2"], v["d2"], u3, d3]
        u_bufs = [*self.h, v["x0"], v["y1"], v["x1"], v["y0"], f0, f1]
        return l_bufs, u_bufs


def body(rows, cols, l_panel, l_rows, u_panel, u_cols, u11_inv, ancestor):
    gz, row, col = (lax.axis_index(a) for a in ("gz", "row", "col"))
    l_own, u_own, inv = l_panel[0, :, 0], u_panel[0, :, 0], u11_inv[0]
    nodes, l_slots = l_own.shape[:2]
    u_slots = u_own.shape[1]
    l_tgt = l_rows[0, :, 0]
    l_tgt = jnp.where(l_tgt < 0, -1, (l_tgt + (AR // 2) * (1 - gz)) % AR)
    u_tgt = u_cols[0, :, 0]
    keep = ancestor[0]

    if rows == 4 and cols == 4:
        half = u_slots // 2
        sources = jnp.stack([col, col - 1, col + 1, col - 2, col + 2, col - 3, col + 3])
        l_base = jnp.where((sources >= 0) & (sources < cols), sources * l_slots, -1)
        squares = jnp.stack([row, row, row ^ 1, row ^ 2, row ^ 1, row ^ 2, row ^ 3, row ^ 3])
        u_base = squares * u_slots + half * jnp.array([0, 1, 0, 1, 1, 0, 0, 1], jnp.int32)
        links = [Link("row"), Link("row"), Link("col"), Link("col")]
        size = 5
        chunks = []
        for here in (slice(0, size), slice(size, nodes)):
            chunks.append(Exchange(links, l_own[here], u_own[here, :half], u_own[here, half:]))
        one, two = chunks
        one.first()
        one.second()
        third = one.third(slice(0, size))
        zero = jnp.zeros((8, 128), F32)

        def run(kernel, chunk, third, here, ls, us, token, held, out, aliases, scratch=(), pin=True):
            l_bufs, u_bufs = chunk.buffers(third)
            tables = [t.astype(jnp.int32) for t in (l_tgt, u_tgt, l_base[ls], u_base[us])]
            l_bufs, u_bufs = l_bufs[ls], u_bufs[us]
            offsets = [here[0] - (0 if chunk is one else size)] * (len(l_bufs) + len(u_bufs))
            return call(
                kernel, here, offsets, tables, l_bufs, u_bufs, inv, token, held, out, aliases, list(scratch), pin
            )

        def cats(count):
            return [pltpu.VMEM((count,) + shape, BF16) for shape in (L_CAT, U_CAT)]

        early, late = (slice(0, 5), slice(0, 6)), (slice(5, 7), slice(6, 8))
        parts = ((0, 3), (3, size))
        held = []
        token = zero
        for here in parts:
            *cat, token = run(
                prepare_kernel, one, third, here, *early, token, (), cats(here[1] - here[0]), {}, (RAW, RAW)
            )
            held.append(cat)
        token = Box(token)
        hold(links, token)
        accs, first = (zero, keep), True
        for stage, here, cat in zip((two.first, two.second), parts, held):
            stage()
            *_, send, keep, token = run(
                functools.partial(finish_kernel, first, (0, 1)),
                one,
                third,
                here,
                *late,
                token.value,
                (*cat, *accs),
                [*cats(here[1] - here[0]), ACC, ACC],
                {0: 0, 1: 1} if first else {0: 0, 1: 1, 2: 2, 3: 3},
            )
            accs, first, token = (send, keep), False, Box(token)
            hold(links, token)
        last = two.third(slice(0, nodes - size))
        here = (size, nodes)
        *cat, token = run(
            prepare_kernel, two, last, here, *early, token.value, (), cats(nodes - size), {}, (RAW, RAW)
        )
        *cat, send, token = run(
            functools.partial(finish_kernel, False, (0,)),
            two,
            last,
            here,
            *late,
            token,
            (*cat, send),
            [*cats(nodes - size), ACC],
            {0: 0, 1: 1, 2: 2},
            pin=False,
        )
        vmem = pl.BlockSpec(memory_space=pltpu.VMEM)
        keep = pl.pallas_call(
            keep_kernel,
            grid=(nodes - size,),
            out_shape=ACC,
            in_specs=[vmem, vmem, pl.BlockSpec(memory_space=pl.ANY), vmem],
            out_specs=vmem,
            input_output_aliases={3: 0},
            compiler_params=PARAMS,
        )(*cat, token, keep)
    else:
        l_all = lax.all_gather(l_own, "col", axis=1, tiled=True)
        u_all = lax.all_gather(u_own, "row", axis=1, tiled=True)
        base, zero = jnp.zeros((1,), jnp.int32), jnp.zeros((8, 128), F32)
        tables = [t.astype(jnp.int32) for t in (l_tgt, u_tgt, base, base)]
        send, keep = apply_update((0, nodes), tables, [l_all], [u_all], inv, zero, keep)

    other = lax.ppermute(send, "gz", [(0, 1), (1, 0)])
    return (keep - other)[None]


def solution(mesh):
    in_specs = (
        P("gz", None, "row", "col", None, None),
        P("gz", None, "row", None),
        P("gz", None, "col", "row", None, None),
        P("gz", None, "col", None),
        P("gz", None, None, None),
        P("row", "gz", "col"),
    )
    return jax.shard_map(
        functools.partial(body, mesh.shape["row"], mesh.shape["col"]),
        mesh=mesh,
        in_specs=in_specs,
        out_specs=P("row", "gz", "col"),
        check_vma=False,
    )
```

```python
import functools

import jax
import jax.numpy as jnp
from jax import lax
from jax.experimental import pallas as pl
from jax.experimental.pallas import tpu as pltpu
from jax.sharding import PartitionSpec as P

W = 256
B = 128
AR = 8
AC = 16
HALF = AR * B // 2
F32 = jnp.float32
BF16 = jnp.bfloat16


def split(x):
    hi = x.astype(BF16)
    return hi, (x - hi.astype(F32)).astype(BF16)


def dot(a, b):
    return jnp.dot(a, b, preferred_element_type=F32)


def slot_rows(l_tgt, l_base, node, b, j):
    base = l_base[b]
    return jnp.where(base >= 0, l_tgt[node, jnp.maximum(base, 0) + j], -1)


def block(tgt):
    return pl.ds(pl.multiple_of(tgt * B, B), B)


def scale(hi, lo, inv):
    return split(dot(hi, inv[0]) + dot(hi, inv[1]) + dot(lo, inv[0]))


def place_l(l_refs, targets, raw_h, raw_l, inv, l_cat):
    raw_h[...] = jnp.zeros_like(raw_h)
    raw_l[...] = jnp.zeros_like(raw_l)
    for b, ref in enumerate(l_refs):
        for j in range(ref.shape[1]):
            tgt = targets(b, j)

            @pl.when(tgt >= 0)
            def _(ref=ref, j=j, tgt=tgt):
                raw_h[block(tgt), :], raw_l[block(tgt), :] = split(ref[0, j])

    for m in range(0, AR * B, 256):
        hi, lo = scale(raw_h[m : m + 256, :], raw_l[m : m + 256, :], inv)
        l_cat[m : m + 256, 0:W] = hi
        l_cat[m : m + 256, W : 2 * W] = lo


def place_u(u_refs, targets, u_cat):
    for b, ref in enumerate(u_refs):
        for j in range(ref.shape[1]):
            tgt = targets(b, j)

            @pl.when(tgt >= 0)
            def _(ref=ref, j=j, tgt=tgt):
                hi, lo = split(ref[0, j])
                u_cat[0:W, block(tgt)] = hi
                u_cat[W : 2 * W, block(tgt)] = lo


def product(l_cat, u_cat, half):
    rows = slice(half * HALF, (half + 1) * HALF)
    lh, ll = l_cat[rows, 0:W], l_cat[rows, W : 2 * W]
    uh, ul = u_cat[0:W, :], u_cat[W : 2 * W, :]
    return dot(lh, uh) + dot(ll, uh) + dot(lh, ul)


def update_kernel(n_l, n_u, start, first, l_tgt, u_tgt, l_base, u_base, *refs):
    l_refs, u_refs, refs = refs[:n_l], refs[n_l : n_l + n_u], refs[n_l + n_u :]
    inv_ref, _, send_in, keep_in, send, keep, token, raw_h, raw_l, l_cat, u_cat = refs
    step = pl.program_id(0)
    node = start + step

    @pl.when(step == 0)
    def _():
        token[...] = jnp.zeros_like(token)
        if first:
            send[...] = jnp.zeros_like(send)
            keep[...] = keep_in[...]

    rows = lambda b, j: slot_rows(l_tgt, l_base, node, b, j)
    place_l(l_refs, rows, raw_h, raw_l, split(inv_ref[0]), l_cat)
    u_cat[...] = jnp.zeros_like(u_cat)
    place_u(u_refs, lambda b, j: u_tgt[node, u_base[b] + j], u_cat)
    send[...] += product(l_cat, u_cat, 0)
    keep[...] -= product(l_cat, u_cat, 1)


def prepare_kernel(n_l, n_u, start, l_tgt, u_tgt, l_base, u_base, *refs):
    l_refs, u_refs, refs = refs[:n_l], refs[n_l : n_l + n_u], refs[n_l + n_u :]
    inv_ref, _, l_cats, u_cats, token, raw_h, raw_l = refs
    step = pl.program_id(0)
    node = start + step
    token[...] = jnp.zeros_like(token)
    rows = lambda b, j: slot_rows(l_tgt, l_base, node, b, j)
    place_l(l_refs, rows, raw_h, raw_l, split(inv_ref[0]), l_cats.at[step])
    u_cats[step] = jnp.zeros(u_cats.shape[1:], BF16)
    place_u(u_refs, lambda b, j: u_tgt[node, u_base[b] + j], u_cats.at[step])


def finish_kernel(first, halves, n_l, n_u, start, l_tgt, u_tgt, l_base, u_base, *refs):
    l_refs, u_refs, refs = refs[:n_l], refs[n_l : n_l + n_u], refs[n_l + n_u :]
    n = len(halves)
    inv_ref, _, refs = refs[0], refs[1], refs[2:]
    ins, (l_cats, u_cats), accs, token = refs[2 : 2 + n], refs[2 + n : 4 + n], refs[4 + n : 4 + 2 * n], refs[-1]
    step = pl.program_id(0)
    node = start + step
    token[...] = jnp.zeros_like(token)
    if first:

        @pl.when(step == 0)
        def _():
            for half, src, acc in zip(halves, ins, accs):
                acc[...] = src[...] if half else jnp.zeros_like(acc)

    l_cat, u_cat = l_cats.at[step], u_cats.at[step]
    add_l(l_refs, lambda b, j: slot_rows(l_tgt, l_base, node, b, j), inv_ref, l_cat)
    place_u(u_refs, lambda b, j: u_tgt[node, u_base[b] + j], u_cat)
    for half, acc in zip(halves, accs):
        part = product(l_cat, u_cat, half)
        acc[...] = acc[...] - part if half else acc[...] + part


def keep_kernel(l_cats, u_cats, _, keep_in, keep):
    step = pl.program_id(0)
    keep[...] -= product(l_cats.at[step], u_cats.at[step], 1)


def add_l(l_refs, targets, inv_ref, l_cat):
    inv = split(inv_ref[0])
    for b, ref in enumerate(l_refs):
        for j in range(ref.shape[1]):
            tgt = targets(b, j)

            @pl.when(tgt >= 0)
            def _(ref=ref, j=j, tgt=tgt):
                hi, lo = scale(*split(ref[0, j]), inv)
                l_cat[block(tgt), 0:W] = hi
                l_cat[block(tgt), W : 2 * W] = lo


RAW = pltpu.VMEM((AR * B, W), BF16)
L_CAT = (AR * B, 2 * W)
U_CAT = (2 * W, AC * B)
PARAMS = pltpu.CompilerParams(dimension_semantics=("arbitrary",), vmem_limit_bytes=20 << 20)


def call(kernel, nodes, offsets, tables, l_bufs, u_bufs, u11_inv, token, held, out, aliases, scratch, pin=True):
    start, stop = nodes

    def per_node(buf, offset):
        return pl.BlockSpec((1,) + buf.shape[1:], lambda s, *_: (offset + s, 0, 0, 0))

    vmem, anywhere = pl.BlockSpec(memory_space=pltpu.VMEM), pl.BlockSpec(memory_space=pl.ANY)
    bufs = [*l_bufs, *u_bufs]
    if pin:
        bufs = [pltpu.with_memory_space_constraint(b, pltpu.HBM) for b in bufs]
    n_in = 6 + len(bufs)
    return pl.pallas_call(
        functools.partial(kernel, len(l_bufs), len(u_bufs), start),
        out_shape=(*out, jax.ShapeDtypeStruct((8, 128), F32)),
        grid_spec=pltpu.PrefetchScalarGridSpec(
            num_scalar_prefetch=4,
            grid=(stop - start,),
            in_specs=[per_node(b, o) for b, o in zip(bufs, offsets)]
            + [pl.BlockSpec((1, W, W), lambda s, *_: (start + s, 0, 0)), anywhere]
            + [vmem] * len(held),
            out_specs=(vmem,) * (len(out) + 1),
            scratch_shapes=scratch,
        ),
        input_output_aliases={n_in + i: o for i, o in aliases.items()},
        compiler_params=PARAMS,
    )(*tables, *bufs, u11_inv, token, *held)


ACC = pltpu.VMEM((HALF, AC * B), F32)


def apply_update(nodes, tables, l_bufs, u_bufs, inv, token, keep):
    kernel = lambda n_l, n_u, start, *refs: update_kernel(n_l, n_u, start, True, *refs)
    scratch = [RAW, RAW, pltpu.VMEM(L_CAT, BF16), pltpu.VMEM(U_CAT, BF16)]
    offsets = [0] * (len(l_bufs) + len(u_bufs))
    send, keep, _ = call(
        kernel, nodes, offsets, tables, l_bufs, u_bufs, inv, token, (token, keep), [ACC] * 2, {}, scratch
    )
    return send, keep


class Box:
    def __init__(self, value):
        self.value = value


def after(x, boxes):
    if not boxes:
        return x
    x, *values = lax.optimization_barrier((x, *[b.value for b in boxes]))
    for box, value in zip(boxes, values):
        box.value = value
    return x


class Link:
    def __init__(self, axis, wait=()):
        self.axis, self.wait = axis, list(wait)

    def send(self, x, pairs):
        out = Box(lax.ppermute(after(x, self.wait), self.axis, pairs))
        self.wait = [out]
        return out


def up(hop):
    return [(z, z + 1) for z in range(hop - 1, 3)]


def down(hop):
    return [(z, z - 1) for z in range(1, 5 - hop)]


def side(mask):
    return [(r, r ^ mask) for r in range(4)]


def hold(links, box):
    for link in links:
        link.wait.append(box)


class Exchange:
    def __init__(self, links, l_chunk, u_h0, u_h1):
        self.links = links
        self.l, self.h = l_chunk, (u_h0, u_h1)

    def first(self):
        lx, ly, lu, ld = self.links
        self.y1, self.x0 = ly.send(self.h[1], side(2)), lx.send(self.h[0], side(1))
        self.d1, self.u1 = ld.send(self.l, down(1)), lu.send(self.l, up(1))

    def second(self):
        lx, ly, lu, ld = self.links
        self.y0, self.x1 = ly.send(self.h[0], side(2)), lx.send(self.h[1], side(1))
        self.d2, self.u2 = ld.send(self.d1.value, down(2)), lu.send(self.u1.value, up(2))

    def third(self, here):
        lx, ly, lu, ld = self.links
        f0, f1 = ly.send(self.x0.value[here], side(2)), lx.send(self.y1.value[here], side(1))
        d3, u3 = ld.send(self.d2.value[here], down(3)), lu.send(self.u2.value[here], up(3))
        return u3, d3, f0, f1

    def buffers(self, third):
        names = ("u1", "d1", "u2", "d2", "x0", "x1", "y0", "y1")
        v = {n: getattr(self, n).value if hasattr(self, n) else None for n in names}
        u3, d3, f0, f1 = (b.value for b in third)
        l_bufs = [self.l, v["u1"], v["d1"], v["u2"], v["d2"], u3, d3]
        u_bufs = [*self.h, v["x0"], v["y1"], v["x1"], v["y0"], f0, f1]
        return l_bufs, u_bufs


def body(rows, cols, l_panel, l_rows, u_panel, u_cols, u11_inv, ancestor):
    gz, row, col = (lax.axis_index(a) for a in ("gz", "row", "col"))
    l_own, u_own, inv = l_panel[0, :, 0], u_panel[0, :, 0], u11_inv[0]
    nodes, l_slots = l_own.shape[:2]
    u_slots = u_own.shape[1]
    l_tgt = l_rows[0, :, 0]
    l_tgt = jnp.where(l_tgt < 0, -1, (l_tgt + (AR // 2) * (1 - gz)) % AR)
    u_tgt = u_cols[0, :, 0]
    keep = ancestor[0]

    if rows == 4 and cols == 4:
        half = u_slots // 2
        sources = jnp.stack([col, col - 1, col + 1, col - 2, col + 2, col - 3, col + 3])
        l_base = jnp.where((sources >= 0) & (sources < cols), sources * l_slots, -1)
        squares = jnp.stack([row, row, row ^ 1, row ^ 2, row ^ 1, row ^ 2, row ^ 3, row ^ 3])
        u_base = squares * u_slots + half * jnp.array([0, 1, 0, 1, 1, 0, 0, 1], jnp.int32)
        links = [Link("row"), Link("row"), Link("col"), Link("col")]
        size = 5
        chunks = []
        for here in (slice(0, size), slice(size, nodes)):
            chunks.append(Exchange(links, l_own[here], u_own[here, :half], u_own[here, half:]))
        one, two = chunks
        one.first()
        one.second()
        third = one.third(slice(0, size))
        zero = jnp.zeros((8, 128), F32)

        def run(kernel, chunk, third, here, ls, us, token, held, out, aliases, scratch=(), pin=True):
            l_bufs, u_bufs = chunk.buffers(third)
            tables = [t.astype(jnp.int32) for t in (l_tgt, u_tgt, l_base[ls], u_base[us])]
            l_bufs, u_bufs = l_bufs[ls], u_bufs[us]
            offsets = [here[0] - (0 if chunk is one else size)] * (len(l_bufs) + len(u_bufs))
            return call(
                kernel, here, offsets, tables, l_bufs, u_bufs, inv, token, held, out, aliases, list(scratch), pin
            )

        def cats(count):
            return [pltpu.VMEM((count,) + shape, BF16) for shape in (L_CAT, U_CAT)]

        early, late = (slice(0, 5), slice(0, 6)), (slice(5, 7), slice(6, 8))
        parts = ((0, 3), (3, size))
        held = []
        token = zero
        for here in parts:
            *cat, token = run(
                prepare_kernel, one, third, here, *early, token, (), cats(here[1] - here[0]), {}, (RAW, RAW)
            )
            held.append(cat)
        token = Box(token)
        hold(links, token)
        accs, first = (zero, keep), True
        for stage, here, cat in zip((two.first, two.second), parts, held):
            stage()
            *_, send, keep, token = run(
                functools.partial(finish_kernel, first, (0, 1)),
                one,
                third,
                here,
                *late,
                token.value,
                (*cat, *accs),
                [*cats(here[1] - here[0]), ACC, ACC],
                {0: 0, 1: 1} if first else {0: 0, 1: 1, 2: 2, 3: 3},
            )
            accs, first, token = (send, keep), False, Box(token)
            hold(links, token)
        last = two.third(slice(0, nodes - size))
        here = (size, nodes)
        *cat, token = run(
            prepare_kernel, two, last, here, *early, token.value, (), cats(nodes - size), {}, (RAW, RAW)
        )
        *cat, send, token = run(
            functools.partial(finish_kernel, False, (0,)),
            two,
            last,
            here,
            *late,
            token,
            (*cat, send),
            [*cats(nodes - size), ACC],
            {0: 0, 1: 1, 2: 2},
            pin=False,
        )
        vmem = pl.BlockSpec(memory_space=pltpu.VMEM)
        keep = pl.pallas_call(
            keep_kernel,
            grid=(nodes - size,),
            out_shape=ACC,
            in_specs=[vmem, vmem, pl.BlockSpec(memory_space=pl.ANY), vmem],
            out_specs=vmem,
            input_output_aliases={3: 0},
            compiler_params=PARAMS,
        )(*cat, token, keep)
    else:
        l_all = lax.all_gather(l_own, "col", axis=1, tiled=True)
        u_all = lax.all_gather(u_own, "row", axis=1, tiled=True)
        base, zero = jnp.zeros((1,), jnp.int32), jnp.zeros((8, 128), F32)
        tables = [t.astype(jnp.int32) for t in (l_tgt, u_tgt, base, base)]
        send, keep = apply_update((0, nodes), tables, [l_all], [u_all], inv, zero, keep)

    other = lax.ppermute(send, "gz", [(0, 1), (1, 0)])
    return (keep - other)[None]


def solution(mesh):
    in_specs = (
        P("gz", None, "row", "col", None, None),
        P("gz", None, "row", None),
        P("gz", None, "col", "row", None, None),
        P("gz", None, "col", None),
        P("gz", None, None, None),
        P("row", "gz", "col"),
    )
    return jax.shard_map(
        functools.partial(body, mesh.shape["row"], mesh.shape["col"]),
        mesh=mesh,
        in_specs=in_specs,
        out_specs=P("row", "gz", "col"),
        check_vma=False,
    )
```
